128 devices in a mesh: pipe: 4 (over x), seq: 32 (over z, y, core).
Axes of the slice: x: 4, y: 4, z: 4, core: 2. Of those that a mesh axis runs over, the one named last changes fastest.
Arguments:
- query_rows: bfloat16 [4, 4096, 1536], P('pipe', 'seq'), may hold values from -6 to 6
- key_rows: bfloat16 [4, 4096, 1536], P('pipe', 'seq'), may hold values from -6 to 6
- value_rows: bfloat16 [4, 4096, 1536], P('pipe', 'seq'), may hold values from -6 to 6
- query_weight: bfloat16 [4, 1536, 1536], P('pipe'), may hold values from -0.15625 to 0.15625
- key_weight: bfloat16 [4, 1536, 1536], P('pipe'), may hold values from -0.15625 to 0.15625
- value_weight: bfloat16 [4, 1536, 1536], P('pipe'), may hold values from -0.15625 to 0.15625
- out_weight: bfloat16 [4, 1536, 1536], P('pipe'), may hold values from -0.15625 to 0.15625
- upstream: bfloat16 [4096, 1536], P('seq'), may hold values from -6 to 6
- window: int32 [32, 12, 2], replicated, may hold values from 0 to 1, as said below
Outputs:
- gradients: bfloat16 [4, 4096, 1536], P('pipe', 'seq')
The draws below stay inside these ranges and needn't reach their ends.
Inputs may be any that keep to these rules, and one draw needn't show every extreme that they name: window[i, h, 0] is 0 where i % 4 == 3, and window[i, h, 1] is 0 where i % 4 == 2.
All inputs are finite; a program needn't handle non-finite values.
Results may differ from the reference program's by a relative error of at most 0.02.
Values may be sent and summed in bfloat16 or wider, within the bound.
A program may use at most 128 MiB of HBM per device.

```python
import jax
import jax.numpy as jnp
from jax import lax

D = 1536
HEADS = 12
HEAD_DIM = 128
TILE = 128
COLUMN = 4
SECTIONS = 4
TILES = 32
TOKENS = 4096
HW = 1536


def draw_query_rows(key, part):
    shape = (SECTIONS, TOKENS, HEADS, HEAD_DIM)
    base = jnp.clip(1.4 * jax.random.normal(jax.random.fold_in(key, 1), shape, jnp.float32), -6.0, 6.0)
    return base.reshape(SECTIONS, TOKENS, HEADS * HEAD_DIM).astype(jnp.bfloat16)


def draw_key_rows(key, part):
    shape = (SECTIONS, TOKENS, HEADS, HEAD_DIM)
    base = jnp.clip(1.4 * jax.random.normal(jax.random.fold_in(key, 2), shape, jnp.float32), -6.0, 6.0)
    return base.reshape(SECTIONS, TOKENS, HEADS * HEAD_DIM).astype(jnp.bfloat16)


def draw_window(key, part):
    level = jax.random.randint(jax.random.fold_in(key, 21), (TILES, 1, 1), 0, 4)
    picks = jax.random.randint(jax.random.fold_in(key, 22), (TILES, HEADS, 2), 0, 3)
    flags = (picks < level).astype(jnp.int32)
    chosen = jax.random.randint(jax.random.fold_in(key, 23), (TILES, 1, 1), 0, HEADS)
    heads = jnp.arange(HEADS)[None, :, None]
    flags = jnp.where(heads == chosen, 1, flags)
    places = jnp.arange(TILES) % COLUMN
    side_before = jnp.where((places == COLUMN - 1)[:, None], 0, flags[:, :, 0])
    side_after = jnp.where((places == COLUMN - 2)[:, None], 0, flags[:, :, 1])
    return jnp.stack([side_before, side_after], axis=-1).astype(jnp.int32)


def level_of(rng, extent, shards, least, largest):
    def one(position, blocks):
        heights = jax.random.uniform(jax.random.fold_in(jax.random.fold_in(rng, 6), position), (blocks,), jnp.float32, least / len(shards), largest / len(shards))
        return jnp.repeat(jnp.exp(heights), extent[position] // blocks).reshape((-1,) + (1,) * (len(extent) - position - 1))

    factor_of = one(*shards[0])
    for cut in shards[1:]:
        factor_of = factor_of * one(*cut)
    return factor_of


def normal_values(key, dims, scale, reach, cuts=(), kind=jnp.bfloat16):
    drawn = jax.random.normal(key, dims, jnp.float32) * scale
    if len(cuts) > 0:
        drawn = level_of(key, dims, cuts, -0.22, 0.18) * drawn
    return jnp.clip(drawn, min=-reach, max=reach).astype(kind)


def setup_inputs(seed: int = 0) -> dict:
    keys = jax.random.split(jax.random.key(seed), 10)
    query_rows = draw_query_rows(jax.random.fold_in(keys[9], 71), 0)
    key_rows = draw_key_rows(jax.random.fold_in(keys[9], 71), 0)
    value_rows = normal_values(keys[2], (SECTIONS, TOKENS, HW), 1.0, 6.0, ((0, 4), (1, 32)))
    query_weight = normal_values(keys[3], (SECTIONS, D, HW), HW ** -0.5, 0.15625, ((0, 4),))
    key_weight = normal_values(keys[4], (SECTIONS, D, HW), HW ** -0.5, 0.15625, ((0, 4),))
    value_weight = normal_values(keys[5], (SECTIONS, D, HW), HW ** -0.5, 0.15625, ((0, 4),))
    out_weight = normal_values(keys[6], (SECTIONS, HW, D), D ** -0.5, 0.15625, ((0, 4),))
    upstream = normal_values(keys[7], (TOKENS, D), 1.0, 6.0, ((0, 32),))
    window = draw_window(jax.random.fold_in(keys[9], 71), 0)
    return {"query_rows": query_rows, "key_rows": key_rows, "value_rows": value_rows, "query_weight": query_weight, "key_weight": key_weight, "value_weight": value_weight, "out_weight": out_weight, "upstream": upstream, "window": window}


def contract_last(first_operand, second_operand):
    return lax.dot_general(first_operand, second_operand, (((1,), (1,)), ((), ())), preferred_element_type=jnp.float32)


def combine_parts(partials):
    empty_tile = jnp.zeros_like(partials[:1, 0])
    from_next = jnp.concatenate([partials[1:, 0], empty_tile], 0)
    from_prev = jnp.concatenate([empty_tile, partials[:-1, 2]], 0)
    return (partials[:, 1] + from_next + from_prev).astype(jnp.bfloat16).reshape(TOKENS, HW)


def section_backward(incoming, query_matrix, key_matrix, value_matrix, out_matrix, queries_all, keys_all, values_all, window):
    scaling = HEAD_DIM ** -0.5
    d_out = contract_last(incoming, out_matrix).astype(jnp.bfloat16)
    tile_shape = (TILES, TILE, HEADS, HEAD_DIM)
    query_tiles = queries_all.reshape(tile_shape)
    out_tiles = d_out.reshape(tile_shape)
    padding = ((1, 1), (0, 0), (0, 0), (0, 0))
    key_padded = jnp.pad(keys_all.reshape(tile_shape), padding)
    value_padded = jnp.pad(values_all.reshape(tile_shape), padding)
    block_shape = (3, TILE, HEADS, HEAD_DIM)

    def one_tile(tile_index):
        tile_index = tile_index.astype(jnp.int32)
        queries = query_tiles[tile_index].astype(jnp.float32)
        grads_out = out_tiles[tile_index].astype(jnp.float32)
        anchor = (tile_index, jnp.int32(0), jnp.int32(0), jnp.int32(0))
        key_block = lax.dynamic_slice(key_padded, anchor, block_shape).reshape(3 * TILE, HEADS, HEAD_DIM).astype(jnp.float32)
        value_block = lax.dynamic_slice(value_padded, anchor, block_shape).reshape(3 * TILE, HEADS, HEAD_DIM).astype(jnp.float32)
        side_flags = window[tile_index] > 0
        keep_mask = jnp.concatenate([jnp.repeat(side_flags[:, 0:1], TILE, axis=1), jnp.ones((HEADS, TILE), dtype=bool), jnp.repeat(side_flags[:, 1:2], TILE, axis=1)], axis=1)
        scores = scaling * jnp.einsum("qhd,khd->hqk", queries, key_block)
        scores = jnp.where(keep_mask[:, None, :], scores, -jnp.inf)
        row_max = jnp.max(scores, axis=-1, keepdims=True)
        log_total = row_max + jnp.log(jnp.sum(jnp.exp(scores - row_max), axis=-1, keepdims=True))
        weights = jnp.exp(scores - log_total)
        weight_change = jnp.einsum("qhd,khd->hqk", grads_out, value_block)
        row_delta = jnp.sum(weights * weight_change, axis=-1, keepdims=True)
        score_change = lax.optimization_barrier((weights * (weight_change - row_delta)).astype(jnp.bfloat16)).astype(jnp.float32)
        weights_low = lax.optimization_barrier(weights.astype(jnp.bfloat16)).astype(jnp.float32)
        query_gradient = (scaling * jnp.einsum("hqk,khd->qhd", score_change, key_block)).astype(jnp.bfloat16)
        key_part = scaling * jnp.einsum("hqk,qhd->khd", score_change, queries)
        value_part = jnp.einsum("hqk,qhd->khd", weights_low, grads_out)
        return query_gradient.reshape(TILE, HW), key_part.reshape(3, TILE, HW), value_part.reshape(3, TILE, HW)

    query_parts, key_parts, value_parts = lax.map(one_tile, jnp.arange(TILES, dtype=jnp.int32))
    query_gradient = query_parts.reshape(TOKENS, HW)
    key_gradient = combine_parts(key_parts)
    value_gradient = combine_parts(value_parts)
    total = incoming.astype(jnp.float32) + contract_last(query_gradient, query_matrix)
    total = total + contract_last(key_gradient, key_matrix) + contract_last(value_gradient, value_matrix)
    return total.astype(jnp.bfloat16)


def reference(query_rows, key_rows, value_rows, query_weight, key_weight, value_weight, out_weight, upstream, window):
    incoming = upstream
    results = []
    for section_index in range(SECTIONS - 1, -1, -1):
        incoming = section_backward(incoming, query_weight[section_index], key_weight[section_index], value_weight[section_index], out_weight[section_index], query_rows[section_index], key_rows[section_index], value_rows[section_index], window)
        results.append(incoming)
    return jnp.stack(results[::-1])
```

```python
import functools

import jax
import jax.numpy as jnp
from jax import lax
from jax.experimental import pallas as pl
from jax.experimental.pallas import tpu as pltpu
from jax.sharding import PartitionSpec as P

HEAD_DIM = 128
COLUMN = 4
CHUNK = 256
MESH = pl.DeviceIdType.MESH
F32 = jnp.float32
BF16 = jnp.bfloat16
LOW = -1e30


def nt(a, b):
    return lax.dot_general(a, b, (((1,), (1,)), ((), ())), preferred_element_type=F32)


def nn(a, b):
    return lax.dot_general(a, b, (((1,), (0,)), ((), ())), preferred_element_type=F32)


def relay_kernel(
    sections, tiles, heads, tile,
    q_hbm, k_hbm, v_hbm, wq_hbm, wk_hbm, wv_hbm, wo_hbm, up_hbm, window_ref,
    out_ref,
    qx, kx, vx, wq, wk, wv, wo, inx, acc, dx, prob, prob_t, mean_v, lsx, dlt, grad, res, stat,
    load_sem, wsem, up_sem,
    kv_send, kv_recv, ls_send, ls_recv, hop_send, hop_recv, fwd_send, fwd_recv, dl_send, dl_recv,
):
    width = q_hbm.shape[2]
    model = up_hbm.shape[1]
    chunks = model // CHUNK
    scaling = HEAD_DIM ** (-0.5)
    stage = lax.axis_index("pipe")
    me = lax.axis_index("seq")
    has_left = jnp.logical_and(lax.rem(me, COLUMN) != COLUMN - 1, me > 0)
    has_right = jnp.logical_and(lax.rem(me, COLUMN) != COLUMN - 2, me < tiles - 1)
    is_first = stage == sections - 1
    sends_on = stage > 0
    own = pl.ds(tile, tile)
    low_rows = pl.ds(0, tile)
    high_rows = pl.ds(2 * tile, tile)
    sides = (
        (0, has_left, {"seq": me - 1}, high_rows),
        (1, has_right, {"seq": me + 1}, low_rows),
    )
    here = ((0, has_left, low_rows), (1, has_right, high_rows))

    barrier = pltpu.get_barrier_semaphore()
    for condition, target in (
        (has_left, {"seq": me - 1}),
        (has_right, {"seq": me + 1}),
        (sends_on, {"pipe": stage - 1}),
        (jnp.logical_not(is_first), {"pipe": stage + 1}),
    ):
        @pl.when(condition)
        def _(target=target):
            pl.semaphore_signal(barrier, inc=1, device_id=target, device_id_type=MESH)

    own_loads = [
        pltpu.make_async_copy(source.at[0], target.at[own], load_sem.at[n])
        for n, (source, target) in enumerate(((k_hbm, kx), (v_hbm, vx), (q_hbm, qx)))
    ]
    for copy in own_loads:
        copy.start()
    weight_loads = [
        pltpu.make_async_copy(source.at[0], target, wsem.at[n])
        for n, (source, target) in enumerate(((wo_hbm, wo), (wq_hbm, wq), (wk_hbm, wk), (wv_hbm, wv)))
    ]
    for n in range(chunks):
        @pl.when(is_first)
        def _(n=n):
            pltpu.make_async_copy(
                up_hbm.at[:, pl.ds(n * CHUNK, CHUNK)], inx.at[n, own], up_sem.at[n]
            ).start()
    for copy in weight_loads:
        copy.start()

    for side, present, rows in here:
        @pl.when(jnp.logical_not(present))
        def _(side=side, rows=rows):
            for ref in (kx, vx, qx):
                ref[rows, :] = jnp.zeros((tile, width), BF16)
            for n in range(chunks):
                inx[n, rows, :] = jnp.zeros((tile, CHUNK), BF16)
            lsx[:, rows] = jnp.zeros((16, tile), F32)
            dlt[:, rows] = jnp.zeros((16, tile), F32)

    one = lambda flag: jnp.where(flag, 1, 0)
    pl.semaphore_wait(
        barrier,
        one(has_left) + one(has_right) + one(sends_on) + one(jnp.logical_not(is_first)),
    )

    def exchange(ordinal, side, target, rows, source, into):
        return pltpu.make_async_remote_copy(
            src_ref=source, dst_ref=into.at[rows],
            send_sem=kv_send.at[ordinal, side], recv_sem=kv_recv.at[ordinal, side],
            device_id=target, device_id_type=MESH,
        )

    statics = ((0, k_hbm, kx), (1, v_hbm, vx), (2, q_hbm, qx))
    for ordinal, source, into in statics:
        for side, present, target, rows in sides:
            @pl.when(present)
            def _(ordinal=ordinal, side=side, target=target, rows=rows, source=source, into=into):
                exchange(ordinal, side, target, rows, source.at[0], into).start()

    def wait_static(ordinal, into):
        for side, present, rows in here:
            @pl.when(present)
            def _(side=side, rows=rows):
                pltpu.make_async_remote_copy(
                    src_ref=into.at[own], dst_ref=into.at[rows],
                    send_sem=kv_send.at[ordinal, 1 - side], recv_sem=kv_recv.at[ordinal, 1 - side],
                    device_id={"seq": me}, device_id_type=MESH,
                ).wait_recv()

    def small_copy(source, into, rows, side, send, recv, target):
        return pltpu.make_async_remote_copy(
            src_ref=source, dst_ref=into.at[:, rows],
            send_sem=send.at[side], recv_sem=recv.at[side],
            device_id=target, device_id_type=MESH,
        )

    def wait_small(into, send, recv):
        for side, present, rows in here:
            @pl.when(present)
            def _(side=side, rows=rows):
                small_copy(into.at[:, own], into, rows, 1 - side, send, recv, {"seq": me}).wait_recv()

    lanes = lax.broadcasted_iota(jnp.int32, (tile, 128), 1)

    def head_cols(h):
        return pl.ds(pl.multiple_of(h * HEAD_DIM, HEAD_DIM), HEAD_DIM)

    def flag(index, h, which):
        return window_ref[index, pl.ds(h, 1), which:which + 1]

    before = jnp.maximum(me - 1, 0)
    after = jnp.minimum(me + 1, tiles - 1)

    for copy in own_loads[:2]:
        copy.wait()
    wait_static(0, kx)
    wait_static(1, vx)

    def forward_head(h, table):
        cols = head_cols(h)
        scores = scaling * nt(qx[own, cols], kx[:, cols])
        left = jnp.where(flag(me, h, 0) > 0, scores[:, :tile], LOW)
        right = jnp.where(flag(me, h, 1) > 0, scores[:, 2 * tile:], LOW)
        scores = jnp.concatenate([left, scores[:, tile:2 * tile], right], axis=1)
        top = jnp.max(scores, axis=1, keepdims=True)
        powers = jnp.exp(scores - top)
        total = jnp.sum(powers, axis=1, keepdims=True)
        weights = powers * (1.0 / total)
        prob[h] = weights
        high = weights.astype(BF16)
        rest = (weights - high.astype(F32)).astype(BF16)
        values = vx[:, cols]
        mean_v[:, cols] = nn(high, values) + nn(rest, values)
        return jnp.where(lanes == h, top + jnp.log(total), table)

    own_loads[2].wait()
    table = lax.fori_loop(0, heads, forward_head, jnp.zeros((tile, 128), F32))
    stat[...] = table.T
    lsx[:, own] = stat[0:16, :]
    for side, present, target, rows in sides:
        @pl.when(present)
        def _(side=side, target=target, rows=rows):
            small_copy(lsx.at[:, own], lsx, rows, side, ls_send, ls_recv, target).start()

    def forward_chunk(n, side, target, rows):
        return pltpu.make_async_remote_copy(
            src_ref=inx.at[n, own], dst_ref=inx.at[n, rows],
            send_sem=fwd_send.at[n, side], recv_sem=fwd_recv.at[n, side],
            device_id=target, device_id_type=MESH,
        )

    def forward_all(n):
        for side, present, target, rows in sides:
            @pl.when(present)
            def _(side=side, target=target, rows=rows):
                forward_chunk(n, side, target, rows).start()

    @pl.when(is_first)
    def _():
        for n in range(chunks):
            pltpu.make_async_copy(
                up_hbm.at[:, pl.ds(n * CHUNK, CHUNK)], inx.at[n, own], up_sem.at[n]
            ).wait()
            forward_all(n)

    acc[...] = jnp.zeros_like(acc)
    wait_static(2, qx)
    wait_small(lsx, ls_send, ls_recv)

    def transposed_head(h, carry):
        cols = head_cols(h)
        scores = scaling * nt(kx[own, cols], qx[:, cols]) - lsx[pl.ds(h, 1), :]
        left_flag = jnp.logical_and(flag(before, h, 1) > 0, me > 0)
        right_flag = jnp.logical_and(flag(after, h, 0) > 0, me < tiles - 1)
        left = jnp.where(left_flag, scores[:, :tile], LOW)
        right = jnp.where(right_flag, scores[:, 2 * tile:], LOW)
        scores = jnp.concatenate([left, scores[:, tile:2 * tile], right], axis=1)
        prob_t[h] = jnp.exp(scores)
        return carry

    lax.fori_loop(0, heads, transposed_head, 0)
    weight_loads[0].wait()

    def hop_copy(n):
        return pltpu.make_async_remote_copy(
            src_ref=res.at[n], dst_ref=inx.at[n, own],
            send_sem=hop_send.at[n], recv_sem=hop_recv.at[n],
            device_id={"pipe": stage - 1}, device_id_type=MESH,
        )

    def wait_forwarded(n):
        for side, present, rows in here:
            @pl.when(present)
            def _(side=side, rows=rows):
                forward_chunk(n, 1 - side, {"seq": me}, rows).wait_recv()

    def accumulate(n):
        k_cols = pl.ds(n * CHUNK, CHUNK)
        last = n == chunks - 1

        @pl.loop(0, width // CHUNK)
        def _(m):
            out_cols = pl.ds(pl.multiple_of(m * CHUNK, CHUNK), CHUNK)
            part = acc[:, out_cols] + nt(inx[n], wo[out_cols, k_cols])
            if last:
                dx[:, out_cols] = part.astype(BF16)
            else:
                acc[:, out_cols] = part

    for n in range(chunks):
        @pl.when(jnp.logical_not(is_first))
        def _(n=n):
            hop_copy(n).wait_recv()
            forward_all(n)
        if n > 0:
            wait_forwarded(n - 1)
            accumulate(n - 1)
    wait_forwarded(chunks - 1)
    accumulate(chunks - 1)

    def delta_head(h, table):
        cols = head_cols(h)
        delta = jnp.sum(dx[own, cols].astype(F32) * mean_v[:, cols], axis=1, keepdims=True)
        return jnp.where(lanes == h, delta, table)

    stat[...] = lax.fori_loop(0, heads, delta_head, jnp.zeros((tile, 128), F32)).T
    dlt[:, own] = stat[0:16, :]
    for side, present, target, rows in sides:
        @pl.when(present)
        def _(side=side, target=target, rows=rows):
            small_copy(dlt.at[:, own], dlt, rows, side, dl_send, dl_recv, target).start()

    def query_head(h, carry):
        cols = head_cols(h)
        d_own = dx[own, cols]
        delta = jnp.sum(d_own.astype(F32) * mean_v[:, cols], axis=1, keepdims=True)
        change = (prob[h] * (nt(d_own, vx[:, cols]) - delta)).astype(BF16)
        grad[0, :, cols] = (scaling * nn(change, kx[:, cols])).astype(BF16)
        grad[2, :, cols] = nn(prob_t[h].astype(BF16), dx[:, cols]).astype(BF16)
        return carry

    lax.fori_loop(0, heads, query_head, 0)
    wait_small(dlt, dl_send, dl_recv)

    def key_head(h, carry):
        cols = head_cols(h)
        change = (prob_t[h] * (nt(vx[own, cols], dx[:, cols]) - dlt[pl.ds(h, 1), :])).astype(BF16)
        grad[1, :, cols] = (scaling * nn(change, qx[:, cols])).astype(BF16)
        return carry

    lax.fori_loop(0, heads, key_head, 0)
    for copy in weight_loads[1:]:
        copy.wait()

    for n in range(chunks):
        rows = pl.ds(n * CHUNK, CHUNK)
        total = inx[n, own, :].astype(F32) + nt(grad[0], wq[rows, :])
        total = total + nt(grad[1], wk[rows, :]) + nt(grad[2], wv[rows, :])
        total = total.astype(BF16)
        res[n] = total

        @pl.when(sends_on)
        def _(n=n):
            hop_copy(n).start()
        out_ref[0, :, rows] = total

    for side, present, target, rows in sides:
        @pl.when(present)
        def _(side=side, target=target, rows=rows):
            for ordinal, source, into in statics:
                exchange(ordinal, side, target, rows, source.at[0], into).wait_send()
            small_copy(lsx.at[:, own], lsx, rows, side, ls_send, ls_recv, target).wait_send()
            small_copy(dlt.at[:, own], dlt, rows, side, dl_send, dl_recv, target).wait_send()
            for n in range(chunks):
                forward_chunk(n, side, target, rows).wait_send()

    @pl.when(sends_on)
    def _():
        for n in range(chunks):
            hop_copy(n).wait_send()


def body(q, k, v, wq, wk, wv, wo, upstream, window):
    sections = lax.axis_size("pipe")
    tiles = window.shape[0]
    heads = window.shape[1]
    tile = q.shape[1]
    width = q.shape[2]
    model = upstream.shape[1]
    chunks = model // CHUNK
    hbm = pl.BlockSpec(memory_space=pl.ANY)
    vmem = pl.BlockSpec(memory_space=pltpu.VMEM)
    dma = pltpu.SemaphoreType.DMA
    return pl.pallas_call(
        functools.partial(relay_kernel, sections, tiles, heads, tile),
        out_shape=jax.ShapeDtypeStruct((1, tile, model), BF16),
        in_specs=[hbm] * 8 + [vmem],
        out_specs=vmem,
        scratch_shapes=[
            pltpu.VMEM((3 * tile, width), BF16),
            pltpu.VMEM((3 * tile, width), BF16),
            pltpu.VMEM((3 * tile, width), BF16),
            pltpu.VMEM((model, width), BF16),
            pltpu.VMEM((model, width), BF16),
            pltpu.VMEM((model, width), BF16),
            pltpu.VMEM((width, model), BF16),
            pltpu.VMEM((chunks, 3 * tile, CHUNK), BF16),
            pltpu.VMEM((3 * tile, width), F32),
            pltpu.VMEM((3 * tile, width), BF16),
            pltpu.VMEM((heads, tile, 3 * tile), F32),
            pltpu.VMEM((heads, tile, 3 * tile), F32),
            pltpu.VMEM((tile, width), F32),
            pltpu.VMEM((16, 3 * tile), F32),
            pltpu.VMEM((16, 3 * tile), F32),
            pltpu.VMEM((3, tile, width), BF16),
            pltpu.VMEM((chunks, tile, CHUNK), BF16),
            pltpu.VMEM((128, tile), F32),
            dma((3,)), dma((4,)), dma((chunks,)),
            dma((3, 2)), dma((3, 2)), dma((2,)), dma((2,)),
            dma((chunks,)), dma((chunks,)), dma((chunks, 2)), dma((chunks, 2)),
            dma((2,)), dma((2,)),
        ],
        compiler_params=pltpu.CompilerParams(
            collective_id=0, has_side_effects=True, vmem_limit_bytes=60 * 1024 * 1024
        ),
    )(q, k, v, wq, wk, wv, wo, upstream, window)


def solution(mesh):
    in_specs = (
        P("pipe", "seq", None),
        P("pipe", "seq", None),
        P("pipe", "seq", None),
        P("pipe", None, None),
        P("pipe", None, None),
        P("pipe", None, None),
        P("pipe", None, None),
        P("seq", None),
        P(),
    )
    out_specs = P("pipe", "seq", None)
    return jax.shard_map(body, mesh=mesh, in_specs=in_specs, out_specs=out_specs, check_vma=False)
```

```python
import functools

import jax
import jax.numpy as jnp
from jax import lax
from jax.experimental import pallas as pl
from jax.experimental.pallas import tpu as pltpu
from jax.sharding import PartitionSpec as P

HEAD_DIM = 128
COLUMN = 4
CHUNK = 256
MESH = pl.DeviceIdType.MESH
F32 = jnp.float32
BF16 = jnp.bfloat16
LOW = -1e30


def nt(a, b):
    return lax.dot_general(a, b, (((1,), (1,)), ((), ())), preferred_element_type=F32)


def nn(a, b):
    return lax.dot_general(a, b, (((1,), (0,)), ((), ())), preferred_element_type=F32)


def relay_kernel(
    sections, tiles, heads, tile,
    q_hbm, k_hbm, v_hbm, wq_hbm, wk_hbm, wv_hbm, wo_hbm, up_hbm, window_ref,
    out_ref,
    qx, kx, vx, wq, wk, wv, wo, inx, acc, dx, prob, prob_t, mean_v, lsx, dlt, grad, res, stat,
    load_sem, wsem, up_sem,
    kv_send, kv_recv, ls_send, ls_recv, hop_send, hop_recv, fwd_send, fwd_recv, dl_send, dl_recv,
):
    width = q_hbm.shape[2]
    model = up_hbm.shape[1]
    chunks = model // CHUNK
    scaling = HEAD_DIM ** (-0.5)
    stage = lax.axis_index("pipe")
    me = lax.axis_index("seq")
    has_left = jnp.logical_and(lax.rem(me, COLUMN) != COLUMN - 1, me > 0)
    has_right = jnp.logical_and(lax.rem(me, COLUMN) != COLUMN - 2, me < tiles - 1)
    is_first = stage == sections - 1
    sends_on = stage > 0
    own = pl.ds(tile, tile)
    low_rows = pl.ds(0, tile)
    high_rows = pl.ds(2 * tile, tile)
    sides = (
        (0, has_left, {"seq": me - 1}, high_rows),
        (1, has_right, {"seq": me + 1}, low_rows),
    )
    here = ((0, has_left, low_rows), (1, has_right, high_rows))

    barrier = pltpu.get_barrier_semaphore()
    for condition, target in (
        (has_left, {"seq": me - 1}),
        (has_right, {"seq": me + 1}),
        (sends_on, {"pipe": stage - 1}),
        (jnp.logical_not(is_first), {"pipe": stage + 1}),
    ):
        @pl.when(condition)
        def _(target=target):
            pl.semaphore_signal(barrier, inc=1, device_id=target, device_id_type=MESH)

    own_loads = [
        pltpu.make_async_copy(source.at[0], target.at[own], load_sem.at[n])
        for n, (source, target) in enumerate(((k_hbm, kx), (v_hbm, vx), (q_hbm, qx)))
    ]
    for copy in own_loads:
        copy.start()
    weight_loads = [
        pltpu.make_async_copy(source.at[0], target, wsem.at[n])
        for n, (source, target) in enumerate(((wo_hbm, wo), (wq_hbm, wq), (wk_hbm, wk), (wv_hbm, wv)))
    ]
    for n in range(chunks):
        @pl.when(is_first)
        def _(n=n):
            pltpu.make_async_copy(
                up_hbm.at[:, pl.ds(n * CHUNK, CHUNK)], inx.at[n, own], up_sem.at[n]
            ).start()
    for copy in weight_loads:
        copy.start()

    for side, present, rows in here:
        @pl.when(jnp.logical_not(present))
        def _(side=side, rows=rows):
            for ref in (kx, vx, qx):
                ref[rows, :] = jnp.zeros((tile, width), BF16)
            for n in range(chunks):
                inx[n, rows, :] = jnp.zeros((tile, CHUNK), BF16)
            lsx[:, rows] = jnp.zeros((16, tile), F32)
            dlt[:, rows] = jnp.zeros((16, tile), F32)

    one = lambda flag: jnp.where(flag, 1, 0)
    pl.semaphore_wait(
        barrier,
        one(has_left) + one(has_right) + one(sends_on) + one(jnp.logical_not(is_first)),
    )

    def exchange(ordinal, side, target, rows, source, into):
        return pltpu.make_async_remote_copy(
            src_ref=source, dst_ref=into.at[rows],
            send_sem=kv_send.at[ordinal, side], recv_sem=kv_recv.at[ordinal, side],
            device_id=target, device_id_type=MESH,
        )

    def forward_chunk(n, side, target, rows):
        return pltpu.make_async_remote_copy(
            src_ref=inx.at[n, own], dst_ref=inx.at[n, rows],
            send_sem=fwd_send.at[n, side], recv_sem=fwd_recv.at[n, side],
            device_id=target, device_id_type=MESH,
        )

    def forward_all(n):
        for side, present, target, rows in sides:
            @pl.when(present)
            def _(side=side, target=target, rows=rows):
                forward_chunk(n, side, target, rows).start()

    statics = ((0, k_hbm, kx), (1, v_hbm, vx), (2, q_hbm, qx))

    def start_static(ordinal, source, into):
        for side, present, target, rows in sides:
            @pl.when(present)
            def _(side=side, target=target, rows=rows):
                exchange(ordinal, side, target, rows, source.at[0], into).start()

    start_static(*statics[0])
    start_static(*statics[1])

    @pl.when(is_first)
    def _():
        for n in range(chunks):
            pltpu.make_async_copy(
                up_hbm.at[:, pl.ds(n * CHUNK, CHUNK)], inx.at[n, own], up_sem.at[n]
            ).wait()
            forward_all(n)

    start_static(*statics[2])

    def wait_static(ordinal, into):
        for side, present, rows in here:
            @pl.when(present)
            def _(side=side, rows=rows):
                pltpu.make_async_remote_copy(
                    src_ref=into.at[own], dst_ref=into.at[rows],
                    send_sem=kv_send.at[ordinal, 1 - side], recv_sem=kv_recv.at[ordinal, 1 - side],
                    device_id={"seq": me}, device_id_type=MESH,
                ).wait_recv()

    def small_copy(source, into, rows, side, send, recv, target):
        return pltpu.make_async_remote_copy(
            src_ref=source, dst_ref=into.at[:, rows],
            send_sem=send.at[side], recv_sem=recv.at[side],
            device_id=target, device_id_type=MESH,
        )

    def wait_small(into, send, recv):
        for side, present, rows in here:
            @pl.when(present)
            def _(side=side, rows=rows):
                small_copy(into.at[:, own], into, rows, 1 - side, send, recv, {"seq": me}).wait_recv()

    lanes = lax.broadcasted_iota(jnp.int32, (tile, 128), 1)

    def head_cols(h):
        if isinstance(h, int):
            return pl.ds(h * HEAD_DIM, HEAD_DIM)
        return pl.ds(pl.multiple_of(h * HEAD_DIM, HEAD_DIM), HEAD_DIM)

    def flag(index, h, which):
        return window_ref[index, pl.ds(h, 1), which:which + 1]

    before = jnp.maximum(me - 1, 0)
    after = jnp.minimum(me + 1, tiles - 1)

    for copy in own_loads[:2]:
        copy.wait()
    wait_static(0, kx)
    wait_static(1, vx)

    def forward_head(h, table):
        cols = head_cols(h)
        scores = scaling * nt(qx[own, cols], kx[:, cols])
        left = jnp.where(flag(me, h, 0) > 0, scores[:, :tile], LOW)
        right = jnp.where(flag(me, h, 1) > 0, scores[:, 2 * tile:], LOW)
        scores = jnp.concatenate([left, scores[:, tile:2 * tile], right], axis=1)
        top = jnp.max(scores, axis=1, keepdims=True)
        powers = jnp.exp(scores - top)
        total = jnp.sum(powers, axis=1, keepdims=True)
        weights = powers * (1.0 / total)
        prob[h] = weights
        high = weights.astype(BF16)
        rest = (weights - high.astype(F32)).astype(BF16)
        values = vx[:, cols]
        mean_v[:, cols] = nn(high, values) + nn(rest, values)
        return jnp.where(lanes == h, top + jnp.log(total), table)

    own_loads[2].wait()
    table = lax.fori_loop(0, heads, forward_head, jnp.zeros((tile, 128), F32), unroll=4)
    stat[...] = table.T
    lsx[:, own] = stat[0:16, :]
    for side, present, target, rows in sides:
        @pl.when(present)
        def _(side=side, target=target, rows=rows):
            small_copy(lsx.at[:, own], lsx, rows, side, ls_send, ls_recv, target).start()

    def transposed_head(h, carry):
        cols = head_cols(h)
        scores = scaling * nt(kx[own, cols], qx[:, cols]) - lsx[pl.ds(h, 1), :]
        left_flag = jnp.logical_and(flag(before, h, 1) > 0, me > 0)
        right_flag = jnp.logical_and(flag(after, h, 0) > 0, me < tiles - 1)
        left = jnp.where(left_flag, scores[:, :tile], LOW)
        right = jnp.where(right_flag, scores[:, 2 * tile:], LOW)
        scores = jnp.concatenate([left, scores[:, tile:2 * tile], right], axis=1)
        prob_t[h] = jnp.exp(scores)
        return carry

    def transposed_all():
        wait_static(2, qx)
        wait_small(lsx, ls_send, ls_recv)
        lax.fori_loop(0, heads, transposed_head, 0, unroll=4)

    pl.when(jnp.logical_not(is_first))(transposed_all)
    weight_loads[0].wait()

    def hop_copy(n):
        return pltpu.make_async_remote_copy(
            src_ref=res.at[n], dst_ref=inx.at[n, own],
            send_sem=hop_send.at[n], recv_sem=hop_recv.at[n],
            device_id={"pipe": stage - 1}, device_id_type=MESH,
        )

    def wait_forwarded(n):
        for side, present, rows in here:
            @pl.when(present)
            def _(side=side, rows=rows):
                forward_chunk(n, 1 - side, {"seq": me}, rows).wait_recv()

    def accumulate(n):
        k_cols = pl.ds(n * CHUNK, CHUNK)
        last = n == chunks - 1

        for m in range(width // CHUNK):
            out_cols = pl.ds(m * CHUNK, CHUNK)
            part = nt(inx[n], wo[out_cols, k_cols])
            if n > 0:
                part = part + acc[:, out_cols]
            if last:
                dx[:, out_cols] = part.astype(BF16)
            else:
                acc[:, out_cols] = part

    for n in range(chunks):
        @pl.when(jnp.logical_not(is_first))
        def _(n=n):
            hop_copy(n).wait_recv()
            forward_all(n)
        if n > 0:
            wait_forwarded(n - 1)
            accumulate(n - 1)
    wait_forwarded(chunks - 1)
    accumulate(chunks - 1)
    pl.when(is_first)(transposed_all)

    def delta_head(h, table):
        cols = head_cols(h)
        delta = jnp.sum(dx[own, cols].astype(F32) * mean_v[:, cols], axis=1, keepdims=True)
        return jnp.where(lanes == h, delta, table)

    table = jnp.zeros((tile, 128), F32)
    for h in range(heads):
        table = delta_head(h, table)
    stat[...] = table.T
    dlt[:, own] = stat[0:16, :]
    for side, present, target, rows in sides:
        @pl.when(present)
        def _(side=side, target=target, rows=rows):
            small_copy(dlt.at[:, own], dlt, rows, side, dl_send, dl_recv, target).start()

    def query_head(h):
        cols = head_cols(h)
        d_own = dx[own, cols]
        delta = jnp.sum(d_own.astype(F32) * mean_v[:, cols], axis=1, keepdims=True)
        change = (prob[h] * (nt(d_own, vx[:, cols]) - delta)).astype(BF16)
        grad[0, :, cols] = (scaling * nn(change, kx[:, cols])).astype(BF16)
        grad[2, :, cols] = nn(prob_t[h].astype(BF16), dx[:, cols]).astype(BF16)

    for h in range(heads):
        query_head(h)
    wait_small(dlt, dl_send, dl_recv)

    def key_head(h):
        cols = head_cols(h)
        change = (prob_t[h] * (nt(vx[own, cols], dx[:, cols]) - dlt[pl.ds(h, 1), :])).astype(BF16)
        grad[1, :, cols] = (scaling * nn(change, qx[:, cols])).astype(BF16)

    for h in range(heads):
        key_head(h)
    for copy in weight_loads[1:]:
        copy.wait()

    for n in range(chunks):
        rows = pl.ds(n * CHUNK, CHUNK)
        total = inx[n, own, :].astype(F32) + nt(grad[0], wq[rows, :])
        total = total + nt(grad[1], wk[rows, :]) + nt(grad[2], wv[rows, :])
        total = total.astype(BF16)
        res[n] = total

        @pl.when(sends_on)
        def _(n=n):
            hop_copy(n).start()
        out_ref[0, :, rows] = total

    for side, present, target, rows in sides:
        @pl.when(present)
        def _(side=side, target=target, rows=rows):
            for ordinal, source, into in statics:
                exchange(ordinal, side, target, rows, source.at[0], into).wait_send()
            small_copy(lsx.at[:, own], lsx, rows, side, ls_send, ls_recv, target).wait_send()
            small_copy(dlt.at[:, own], dlt, rows, side, dl_send, dl_recv, target).wait_send()
            for n in range(chunks):
                forward_chunk(n, side, target, rows).wait_send()

    @pl.when(sends_on)
    def _():
        for n in range(chunks):
            hop_copy(n).wait_send()


def body(q, k, v, wq, wk, wv, wo, upstream, window):
    sections = lax.axis_size("pipe")
    tiles = window.shape[0]
    heads = window.shape[1]
    tile = q.shape[1]
    width = q.shape[2]
    model = upstream.shape[1]
    chunks = model // CHUNK
    hbm = pl.BlockSpec(memory_space=pl.ANY)
    vmem = pl.BlockSpec(memory_space=pltpu.VMEM)
    dma = pltpu.SemaphoreType.DMA
    return pl.pallas_call(
        functools.partial(relay_kernel, sections, tiles, heads, tile),
        out_shape=jax.ShapeDtypeStruct((1, tile, model), BF16),
        in_specs=[hbm] * 8 + [vmem],
        out_specs=vmem,
        scratch_shapes=[
            pltpu.VMEM((3 * tile, width), BF16),
            pltpu.VMEM((3 * tile, width), BF16),
            pltpu.VMEM((3 * tile, width), BF16),
            pltpu.VMEM((model, width), BF16),
            pltpu.VMEM((model, width), BF16),
            pltpu.VMEM((model, width), BF16),
            pltpu.VMEM((width, model), BF16),
            pltpu.VMEM((chunks, 3 * tile, CHUNK), BF16),
            pltpu.VMEM((3 * tile, width), F32),
            pltpu.VMEM((3 * tile, width), BF16),
            pltpu.VMEM((heads, tile, 3 * tile), F32),
            pltpu.VMEM((heads, tile, 3 * tile), F32),
            pltpu.VMEM((tile, width), F32),
            pltpu.VMEM((16, 3 * tile), F32),
            pltpu.VMEM((16, 3 * tile), F32),
            pltpu.VMEM((3, tile, width), BF16),
            pltpu.VMEM((chunks, tile, CHUNK), BF16),
            pltpu.VMEM((128, tile), F32),
            dma((3,)), dma((4,)), dma((chunks,)),
            dma((3, 2)), dma((3, 2)), dma((2,)), dma((2,)),
            dma((chunks,)), dma((chunks,)), dma((chunks, 2)), dma((chunks, 2)),
            dma((2,)), dma((2,)),
        ],
        compiler_params=pltpu.CompilerParams(
            collective_id=0, has_side_effects=True, vmem_limit_bytes=60 * 1024 * 1024
        ),
    )(q, k, v, wq, wk, wv, wo, upstream, window)


def solution(mesh):
    in_specs = (
        P("pipe", "seq", None),
        P("pipe", "seq", None),
        P("pipe", "seq", None),
        P("pipe", None, None),
        P("pipe", None, None),
        P("pipe", None, None),
        P("pipe", None, None),
        P("seq", None),
        P(),
    )
    out_specs = P("pipe", "seq", None)
    return jax.shard_map(body, mesh=mesh, in_specs=in_specs, out_specs=out_specs, check_vma=False)
```

```python
import functools

import jax
import jax.numpy as jnp
from jax import lax
from jax.experimental import pallas as pl
from jax.experimental.pallas import tpu as pltpu
from jax.sharding import PartitionSpec as P

HEAD_DIM = 128
COLUMN = 4
CHUNK = 256
LAG = 2
MESH = pl.DeviceIdType.MESH
F32 = jnp.float32
BF16 = jnp.bfloat16
LOW = -1e30


def nt(a, b):
    return lax.dot_general(a, b, (((1,), (1,)), ((), ())), preferred_element_type=F32)


def nn(a, b):
    return lax.dot_general(a, b, (((1,), (0,)), ((), ())), preferred_element_type=F32)


def relay_kernel(
    sections, tiles, heads, tile,
    q_hbm, k_hbm, v_hbm, wq_hbm, wk_hbm, wv_hbm, wo_hbm, up_hbm, window_ref,
    out_ref,
    qx, kx, vx, wq, wk, wv, wo, inx, acc, dx, prob, prob_t, mean_v, lsx, dlt, grad, res, stat,
    load_sem, wsem, up_sem,
    kv_send, kv_recv, ls_send, ls_recv, hop_send, hop_recv, fwd_send, fwd_recv, dl_send, dl_recv,
):
    width = q_hbm.shape[2]
    model = up_hbm.shape[1]
    chunks = model // CHUNK
    scaling = HEAD_DIM ** (-0.5)
    stage = lax.axis_index("pipe")
    me = lax.axis_index("seq")
    has_left = jnp.logical_and(lax.rem(me, COLUMN) != COLUMN - 1, me > 0)
    has_right = jnp.logical_and(lax.rem(me, COLUMN) != COLUMN - 2, me < tiles - 1)
    is_first = stage == sections - 1
    sends_on = stage > 0
    own = pl.ds(tile, tile)
    low_rows = pl.ds(0, tile)
    high_rows = pl.ds(2 * tile, tile)
    sides = (
        (0, has_left, {"seq": me - 1}, high_rows),
        (1, has_right, {"seq": me + 1}, low_rows),
    )
    here = ((0, has_left, low_rows), (1, has_right, high_rows))

    barrier = pltpu.get_barrier_semaphore()
    for condition, target in (
        (has_left, {"seq": me - 1}),
        (has_right, {"seq": me + 1}),
        (sends_on, {"pipe": stage - 1}),
        (jnp.logical_not(is_first), {"pipe": stage + 1}),
    ):
        @pl.when(condition)
        def _(target=target):
            pl.semaphore_signal(barrier, inc=1, device_id=target, device_id_type=MESH)

    own_loads = [
        pltpu.make_async_copy(source.at[0], target.at[own], load_sem.at[n])
        for n, (source, target) in enumerate(((k_hbm, kx), (v_hbm, vx), (q_hbm, qx)))
    ]
    for copy in own_loads:
        copy.start()
    weight_loads = [
        pltpu.make_async_copy(source.at[0], target, wsem.at[n])
        for n, (source, target) in enumerate(((wo_hbm, wo), (wq_hbm, wq), (wk_hbm, wk), (wv_hbm, wv)))
    ]
    for n in range(chunks):
        @pl.when(is_first)
        def _(n=n):
            pltpu.make_async_copy(
                up_hbm.at[:, pl.ds(n * CHUNK, CHUNK)], inx.at[n, own], up_sem.at[n]
            ).start()
    for copy in weight_loads:
        copy.start()

    for side, present, rows in here:
        @pl.when(jnp.logical_not(present))
        def _(side=side, rows=rows):
            for ref in (kx, vx, qx):
                ref[rows, :] = jnp.zeros((tile, width), BF16)
            for n in range(chunks):
                inx[n, rows, :] = jnp.zeros((tile, CHUNK), BF16)
            lsx[:, rows] = jnp.zeros((16, tile), F32)
            dlt[:, rows] = jnp.zeros((16, tile), F32)

    one = lambda flag: jnp.where(flag, 1, 0)
    pl.semaphore_wait(
        barrier,
        one(has_left) + one(has_right) + one(sends_on) + one(jnp.logical_not(is_first)),
    )

    def exchange(ordinal, side, target, rows, source, into):
        return pltpu.make_async_remote_copy(
            src_ref=source, dst_ref=into.at[rows],
            send_sem=kv_send.at[ordinal, side], recv_sem=kv_recv.at[ordinal, side],
            device_id=target, device_id_type=MESH,
        )

    def forward_chunk(n, side, target, rows):
        return pltpu.make_async_remote_copy(
            src_ref=inx.at[n, own], dst_ref=inx.at[n, rows],
            send_sem=fwd_send.at[n, side], recv_sem=fwd_recv.at[n, side],
            device_id=target, device_id_type=MESH,
        )

    def forward_all(n):
        for side, present, target, rows in sides:
            @pl.when(present)
            def _(side=side, target=target, rows=rows):
                forward_chunk(n, side, target, rows).start()

    statics = ((0, k_hbm, kx), (1, v_hbm, vx), (2, q_hbm, qx))

    def start_static(ordinal, source, into):
        for side, present, target, rows in sides:
            @pl.when(present)
            def _(side=side, target=target, rows=rows):
                exchange(ordinal, side, target, rows, source.at[0], into).start()

    start_static(*statics[0])
    start_static(*statics[1])

    @pl.when(is_first)
    def _():
        for n in range(chunks):
            pltpu.make_async_copy(
                up_hbm.at[:, pl.ds(n * CHUNK, CHUNK)], inx.at[n, own], up_sem.at[n]
            ).wait()
            forward_all(n)

    start_static(*statics[2])

    def wait_static(ordinal, into):
        for side, present, rows in here:
            @pl.when(present)
            def _(side=side, rows=rows):
                pltpu.make_async_remote_copy(
                    src_ref=into.at[own], dst_ref=into.at[rows],
                    send_sem=kv_send.at[ordinal, 1 - side], recv_sem=kv_recv.at[ordinal, 1 - side],
                    device_id={"seq": me}, device_id_type=MESH,
                ).wait_recv()

    def small_copy(source, into, rows, side, send, recv, target):
        return pltpu.make_async_remote_copy(
            src_ref=source, dst_ref=into.at[:, rows],
            send_sem=send.at[side], recv_sem=recv.at[side],
            device_id=target, device_id_type=MESH,
        )

    def wait_small(into, send, recv):
        for side, present, rows in here:
            @pl.when(present)
            def _(side=side, rows=rows):
                small_copy(into.at[:, own], into, rows, 1 - side, send, recv, {"seq": me}).wait_recv()

    lanes = lax.broadcasted_iota(jnp.int32, (tile, 128), 1)

    def head_cols(h):
        if isinstance(h, int):
            return pl.ds(h * HEAD_DIM, HEAD_DIM)
        return pl.ds(pl.multiple_of(h * HEAD_DIM, HEAD_DIM), HEAD_DIM)

    def flag(index, h, which):
        return window_ref[index, pl.ds(h, 1), which:which + 1]

    before = jnp.maximum(me - 1, 0)
    after = jnp.minimum(me + 1, tiles - 1)

    for copy in own_loads[:2]:
        copy.wait()
    wait_static(0, kx)
    wait_static(1, vx)

    def forward_head(h, table):
        cols = head_cols(h)
        scores = scaling * nt(qx[own, cols], kx[:, cols])
        left = jnp.where(flag(me, h, 0) > 0, scores[:, :tile], LOW)
        right = jnp.where(flag(me, h, 1) > 0, scores[:, 2 * tile:], LOW)
        scores = jnp.concatenate([left, scores[:, tile:2 * tile], right], axis=1)
        top = jnp.max(scores, axis=1, keepdims=True)
        powers = jnp.exp(scores - top)
        total = jnp.sum(powers, axis=1, keepdims=True)
        weights = powers * (1.0 / total)
        prob[h] = weights
        high = weights.astype(BF16)
        rest = (weights - high.astype(F32)).astype(BF16)
        values = vx[:, cols]
        mean_v[:, cols] = nn(high, values) + nn(rest, values)
        return jnp.where(lanes == h, top + jnp.log(total), table)

    own_loads[2].wait()
    table = lax.fori_loop(0, heads, forward_head, jnp.zeros((tile, 128), F32), unroll=4)
    stat[...] = table.T
    lsx[:, own] = stat[0:16, :]
    for side, present, target, rows in sides:
        @pl.when(present)
        def _(side=side, target=target, rows=rows):
            small_copy(lsx.at[:, own], lsx, rows, side, ls_send, ls_recv, target).start()

    def transposed_head(h, carry):
        cols = head_cols(h)
        scores = scaling * nt(kx[own, cols], qx[:, cols]) - lsx[pl.ds(h, 1), :]
        left_flag = jnp.logical_and(flag(before, h, 1) > 0, me > 0)
        right_flag = jnp.logical_and(flag(after, h, 0) > 0, me < tiles - 1)
        left = jnp.where(left_flag, scores[:, :tile], LOW)
        right = jnp.where(right_flag, scores[:, 2 * tile:], LOW)
        scores = jnp.concatenate([left, scores[:, tile:2 * tile], right], axis=1)
        prob_t[h] = jnp.exp(scores)
        return carry

    def transposed_all():
        wait_static(2, qx)
        wait_small(lsx, ls_send, ls_recv)
        lax.fori_loop(0, heads, transposed_head, 0, unroll=4)

    pl.when(jnp.logical_not(is_first))(transposed_all)
    weight_loads[0].wait()

    def hop_copy(n):
        return pltpu.make_async_remote_copy(
            src_ref=res.at[n], dst_ref=inx.at[n, own],
            send_sem=hop_send.at[n], recv_sem=hop_recv.at[n],
            device_id={"pipe": stage - 1}, device_id_type=MESH,
        )

    def wait_forwarded(n):
        for side, present, rows in here:
            @pl.when(present)
            def _(side=side, rows=rows):
                forward_chunk(n, 1 - side, {"seq": me}, rows).wait_recv()

    def accumulate(n, row_sets):
        rows_in = [inx[n, rows, :] for rows in row_sets]
        incoming = rows_in[0] if len(rows_in) == 1 else jnp.concatenate(rows_in, axis=0)
        for m in range(width // CHUNK):
            out_cols = pl.ds(m * CHUNK, CHUNK)
            product = nt(incoming, wo[out_cols, pl.ds(n * CHUNK, CHUNK)])
            for i, rows in enumerate(row_sets):
                part = product[i * tile:(i + 1) * tile]
                if n > 0:
                    part = part + acc[rows, out_cols]
                if n == chunks - 1:
                    dx[rows, out_cols] = part.astype(BF16)
                else:
                    acc[rows, out_cols] = part

    def accumulate_halo(n):
        wait_forwarded(n)
        accumulate(n, (low_rows, high_rows))

    for n in range(chunks):
        if n >= LAG:
            accumulate_halo(n - LAG)

        @pl.when(jnp.logical_not(is_first))
        def _(n=n):
            hop_copy(n).wait_recv()
            forward_all(n)
        accumulate(n, (own,))

    def delta_head(h, table):
        cols = head_cols(h)
        delta = jnp.sum(dx[own, cols].astype(F32) * mean_v[:, cols], axis=1, keepdims=True)
        return jnp.where(lanes == h, delta, table)

    table = jnp.zeros((tile, 128), F32)
    for h in range(heads):
        table = delta_head(h, table)
    stat[...] = table.T
    dlt[:, own] = stat[0:16, :]
    for side, present, target, rows in sides:
        @pl.when(present)
        def _(side=side, target=target, rows=rows):
            small_copy(dlt.at[:, own], dlt, rows, side, dl_send, dl_recv, target).start()

    def query_head(h):
        cols = head_cols(h)
        d_own = dx[own, cols]
        delta = jnp.sum(d_own.astype(F32) * mean_v[:, cols], axis=1, keepdims=True)
        change = (prob[h] * (nt(d_own, vx[:, cols]) - delta)).astype(BF16)
        grad[0, :, cols] = (scaling * nn(change, kx[:, cols])).astype(BF16)

    for h in range(heads):
        query_head(h)
    for n in range(chunks - LAG, chunks):
        accumulate_halo(n)
    pl.when(is_first)(transposed_all)
    wait_small(dlt, dl_send, dl_recv)

    def key_head(h):
        cols = head_cols(h)
        grad[2, :, cols] = nn(prob_t[h].astype(BF16), dx[:, cols]).astype(BF16)
        change = (prob_t[h] * (nt(vx[own, cols], dx[:, cols]) - dlt[pl.ds(h, 1), :])).astype(BF16)
        grad[1, :, cols] = (scaling * nn(change, qx[:, cols])).astype(BF16)

    for h in range(heads):
        key_head(h)
    for copy in weight_loads[1:]:
        copy.wait()

    for n in range(chunks):
        rows = pl.ds(n * CHUNK, CHUNK)
        total = inx[n, own, :].astype(F32) + nt(grad[0], wq[rows, :])
        total = total + nt(grad[1], wk[rows, :]) + nt(grad[2], wv[rows, :])
        total = total.astype(BF16)
        res[n] = total

        @pl.when(sends_on)
        def _(n=n):
            hop_copy(n).start()
        out_ref[0, :, rows] = total

    for side, present, target, rows in sides:
        @pl.when(present)
        def _(side=side, target=target, rows=rows):
            for ordinal, source, into in statics:
                exchange(ordinal, side, target, rows, source.at[0], into).wait_send()
            small_copy(lsx.at[:, own], lsx, rows, side, ls_send, ls_recv, target).wait_send()
            small_copy(dlt.at[:, own], dlt, rows, side, dl_send, dl_recv, target).wait_send()
            for n in range(chunks):
                forward_chunk(n, side, target, rows).wait_send()

    @pl.when(sends_on)
    def _():
        for n in range(chunks):
            hop_copy(n).wait_send()


def body(q, k, v, wq, wk, wv, wo, upstream, window):
    sections = lax.axis_size("pipe")
    tiles = window.shape[0]
    heads = window.shape[1]
    tile = q.shape[1]
    width = q.shape[2]
    model = upstream.shape[1]
    chunks = model // CHUNK
    hbm = pl.BlockSpec(memory_space=pl.ANY)
    vmem = pl.BlockSpec(memory_space=pltpu.VMEM)
    dma = pltpu.SemaphoreType.DMA
    return pl.pallas_call(
        functools.partial(relay_kernel, sections, tiles, heads, tile),
        out_shape=jax.ShapeDtypeStruct((1, tile, model), BF16),
        in_specs=[hbm] * 8 + [vmem],
        out_specs=vmem,
        scratch_shapes=[
            pltpu.VMEM((3 * tile, width), BF16),
            pltpu.VMEM((3 * tile, width), BF16),
            pltpu.VMEM((3 * tile, width), BF16),
            pltpu.VMEM((model, width), BF16),
            pltpu.VMEM((model, width), BF16),
            pltpu.VMEM((model, width), BF16),
            pltpu.VMEM((width, model), BF16),
            pltpu.VMEM((chunks, 3 * tile, CHUNK), BF16),
            pltpu.VMEM((3 * tile, width), F32),
            pltpu.VMEM((3 * tile, width), BF16),
            pltpu.VMEM((heads, tile, 3 * tile), F32),
            pltpu.VMEM((heads, tile, 3 * tile), F32),
            pltpu.VMEM((tile, width), F32),
            pltpu.VMEM((16, 3 * tile), F32),
            pltpu.VMEM((16, 3 * tile), F32),
            pltpu.VMEM((3, tile, width), BF16),
            pltpu.VMEM((chunks, tile, CHUNK), BF16),
            pltpu.VMEM((128, tile), F32),
            dma((3,)), dma((4,)), dma((chunks,)),
            dma((3, 2)), dma((3, 2)), dma((2,)), dma((2,)),
            dma((chunks,)), dma((chunks,)), dma((chunks, 2)), dma((chunks, 2)),
            dma((2,)), dma((2,)),
        ],
        compiler_params=pltpu.CompilerParams(
            collective_id=0, has_side_effects=True, vmem_limit_bytes=60 * 1024 * 1024
        ),
    )(q, k, v, wq, wk, wv, wo, upstream, window)


def solution(mesh):
    in_specs = (
        P("pipe", "seq", None),
        P("pipe", "seq", None),
        P("pipe", "seq", None),
        P("pipe", None, None),
        P("pipe", None, None),
        P("pipe", None, None),
        P("pipe", None, None),
        P("seq", None),
        P(),
    )
    out_specs = P("pipe", "seq", None)
    return jax.shard_map(body, mesh=mesh, in_specs=in_specs, out_specs=out_specs, check_vma=False)
```

```python
import functools

import jax
import jax.numpy as jnp
from jax import lax
from jax.experimental import pallas as pl
from jax.experimental.pallas import tpu as pltpu
from jax.sharding import PartitionSpec as P

HEAD_DIM = 128
COLUMN = 4
CHUNK = 256
LAG = 2
GROUPS = 3
MESH = pl.DeviceIdType.MESH
F32 = jnp.float32
BF16 = jnp.bfloat16
LOW = -1e30


def nt(a, b):
    return lax.dot_general(a, b, (((1,), (1,)), ((), ())), preferred_element_type=F32)


def nn(a, b):
    return lax.dot_general(a, b, (((1,), (0,)), ((), ())), preferred_element_type=F32)


def relay_kernel(
    sections, tiles, heads, tile,
    q_hbm, k_hbm, v_hbm, wq_hbm, wk_hbm, wv_hbm, wo_hbm, up_hbm, window_hbm,
    out_ref,
    qx, kx, vx, wq, wk, wv, wo, inx, acc, dx, prob, prob_t, mean_v, lsx, dlt, grad, res, stat, window, flags,
    load_sem, wsem, up_sem,
    kv_send, kv_recv, ls_send, ls_recv, hop_send, hop_recv, fwd_send, fwd_recv, dl_send, dl_recv,
):
    width = q_hbm.shape[2]
    model = up_hbm.shape[1]
    chunks = model // CHUNK
    scaling = HEAD_DIM ** (-0.5)
    stage = lax.axis_index("pipe")
    me = lax.axis_index("seq")
    has_left = jnp.logical_and(lax.rem(me, COLUMN) != COLUMN - 1, me > 0)
    has_right = jnp.logical_and(lax.rem(me, COLUMN) != COLUMN - 2, me < tiles - 1)
    is_first = stage == sections - 1
    sends_on = stage > 0
    own = pl.ds(tile, tile)
    low_rows = pl.ds(0, tile)
    high_rows = pl.ds(2 * tile, tile)
    sides = (
        (0, has_left, {"seq": me - 1}, high_rows),
        (1, has_right, {"seq": me + 1}, low_rows),
    )
    here = ((0, has_left, low_rows), (1, has_right, high_rows))

    barrier = pltpu.get_barrier_semaphore()
    for condition, target in (
        (has_left, {"seq": me - 1}),
        (has_right, {"seq": me + 1}),
        (sends_on, {"pipe": stage - 1}),
        (jnp.logical_not(is_first), {"pipe": stage + 1}),
    ):
        @pl.when(condition)
        def _(target=target):
            pl.semaphore_signal(barrier, inc=1, device_id=target, device_id_type=MESH)

    own_loads = [
        pltpu.make_async_copy(source.at[0], target.at[own], load_sem.at[n])
        for n, (source, target) in enumerate(((k_hbm, kx), (v_hbm, vx), (q_hbm, qx)))
    ]
    window_load = pltpu.make_async_copy(window_hbm, window, load_sem.at[3])
    window_load.start()
    for copy in own_loads:
        copy.start()
    weight_loads = [
        pltpu.make_async_copy(source.at[0], target, wsem.at[n])
        for n, (source, target) in enumerate(((wo_hbm, wo), (wq_hbm, wq), (wk_hbm, wk), (wv_hbm, wv)))
    ]
    for n in range(chunks):
        @pl.when(is_first)
        def _(n=n):
            pltpu.make_async_copy(
                up_hbm.at[:, pl.ds(n * CHUNK, CHUNK)], inx.at[n, own], up_sem.at[n]
            ).start()
    for copy in weight_loads:
        copy.start()

    for side, present, rows in here:
        @pl.when(jnp.logical_not(present))
        def _(side=side, rows=rows):
            for ref in (kx, vx, qx):
                ref[rows, :] = jnp.zeros((tile, width), BF16)
            for n in range(chunks):
                inx[n, rows, :] = jnp.zeros((tile, CHUNK), BF16)
            lsx[:, rows] = jnp.zeros((16, tile), F32)
            dlt[:, rows] = jnp.zeros((16, tile), F32)

    one = lambda flag: jnp.where(flag, 1, 0)
    pl.semaphore_wait(
        barrier,
        one(has_left) + one(has_right) + one(sends_on) + one(jnp.logical_not(is_first)),
    )

    def exchange(ordinal, side, target, rows, cols, source, into):
        return pltpu.make_async_remote_copy(
            src_ref=source.at[0, :, cols], dst_ref=into.at[rows, cols],
            send_sem=kv_send.at[ordinal, side], recv_sem=kv_recv.at[ordinal, side],
            device_id=target, device_id_type=MESH,
        )

    def forward_chunk(n, side, target, rows):
        return pltpu.make_async_remote_copy(
            src_ref=inx.at[n, own], dst_ref=inx.at[n, rows],
            send_sem=fwd_send.at[n, side], recv_sem=fwd_recv.at[n, side],
            device_id=target, device_id_type=MESH,
        )

    def forward_all(n):
        for side, present, target, rows in sides:
            @pl.when(present)
            def _(side=side, target=target, rows=rows):
                forward_chunk(n, side, target, rows).start()

    group = heads // GROUPS
    every = pl.ds(0, width)
    statics = [(0, every, k_hbm, kx), (1, every, v_hbm, vx)] + [
        (2 + g, pl.ds(g * group * HEAD_DIM, group * HEAD_DIM), q_hbm, qx) for g in range(GROUPS)
    ]

    def start_static(ordinal):
        _, cols, source, into = statics[ordinal]
        for side, present, target, rows in sides:
            @pl.when(present)
            def _(side=side, target=target, rows=rows):
                exchange(ordinal, side, target, rows, cols, source, into).start()

    start_static(0)
    start_static(1)

    @pl.when(is_first)
    def _():
        for n in range(chunks):
            pltpu.make_async_copy(
                up_hbm.at[:, pl.ds(n * CHUNK, CHUNK)], inx.at[n, own], up_sem.at[n]
            ).wait()
            forward_all(n)

    def wait_static(ordinal):
        _, cols, _, into = statics[ordinal]
        for side, present, rows in here:
            @pl.when(present)
            def _(side=side, rows=rows):
                pltpu.make_async_remote_copy(
                    src_ref=into.at[own, cols], dst_ref=into.at[rows, cols],
                    send_sem=kv_send.at[ordinal, 1 - side], recv_sem=kv_recv.at[ordinal, 1 - side],
                    device_id={"seq": me}, device_id_type=MESH,
                ).wait_recv()

    def small_copy(source, into, rows, side, send, recv, target):
        return pltpu.make_async_remote_copy(
            src_ref=source, dst_ref=into.at[:, rows],
            send_sem=send.at[side], recv_sem=recv.at[side],
            device_id=target, device_id_type=MESH,
        )

    def wait_small(into, send, recv):
        for side, present, rows in here:
            @pl.when(present)
            def _(side=side, rows=rows):
                small_copy(into.at[:, own], into, rows, 1 - side, send, recv, {"seq": me}).wait_recv()

    lanes = lax.broadcasted_iota(jnp.int32, (tile, 128), 1)

    def head_cols(h):
        if isinstance(h, int):
            return pl.ds(h * HEAD_DIM, HEAD_DIM)
        return pl.ds(pl.multiple_of(h * HEAD_DIM, HEAD_DIM), HEAD_DIM)

    def flag(kind, h):
        return flags[kind, pl.ds(h, 1), 0:1]

    before = jnp.maximum(me - 1, 0)
    after = jnp.minimum(me + 1, tiles - 1)

    def accumulate(n, row_sets):
        rows_in = [inx[n, rows, :] for rows in row_sets]
        incoming = rows_in[0] if len(rows_in) == 1 else jnp.concatenate(rows_in, axis=0)
        for m in range(width // CHUNK):
            out_cols = pl.ds(m * CHUNK, CHUNK)
            product = nt(incoming, wo[out_cols, pl.ds(n * CHUNK, CHUNK)])
            for i, rows in enumerate(row_sets):
                part = product[i * tile:(i + 1) * tile]
                if n > 0:
                    part = part + acc[rows, out_cols]
                if n == chunks - 1:
                    dx[rows, out_cols] = part.astype(BF16)
                else:
                    acc[rows, out_cols] = part

    @pl.when(is_first)
    def _():
        weight_loads[0].wait()
        for n in range(chunks):
            accumulate(n, (own,))

    window_load.wait()
    places = lax.broadcasted_iota(jnp.int32, (heads, tiles), 1)
    for kind, (index, which) in enumerate(((me, 0), (me, 1), (before, 1), (after, 0))):
        picked = jnp.where(places == index, window[:, which, :], 0).astype(F32)
        picked = jnp.sum(picked, axis=1, keepdims=True)
        flags[kind, 0:heads, :] = jnp.broadcast_to(picked, (heads, 128))

    for copy in own_loads:
        copy.wait()
    wait_static(0)

    def forward_head(h, table):
        cols = head_cols(h)
        scores = scaling * nt(qx[own, cols], kx[:, cols])
        left = jnp.where(flag(0, h) > 0, scores[:, :tile], LOW)
        right = jnp.where(flag(1, h) > 0, scores[:, 2 * tile:], LOW)
        scores = jnp.concatenate([left, scores[:, tile:2 * tile], right], axis=1)
        top = jnp.max(scores, axis=1, keepdims=True)
        powers = jnp.exp(scores - top)
        total = jnp.sum(powers, axis=1, keepdims=True)
        prob[h] = powers * (1.0 / total)
        return jnp.where(lanes == h, top + jnp.log(total), table)

    def mean_head(h, carry):
        cols = head_cols(h)
        weights = prob[h]
        high = weights.astype(BF16)
        rest = (weights - high.astype(F32)).astype(BF16)
        values = vx[:, cols]
        mean_v[:, cols] = nn(high, values) + nn(rest, values)
        return carry

    table = lax.fori_loop(0, heads, forward_head, jnp.zeros((tile, 128), F32), unroll=4)
    stat[...] = table.T
    lsx[:, own] = stat[0:16, :]
    for side, present, target, rows in sides:
        @pl.when(present)
        def _(side=side, target=target, rows=rows):
            small_copy(lsx.at[:, own], lsx, rows, side, ls_send, ls_recv, target).start()

    start_static(2)
    wait_static(1)
    lax.fori_loop(0, heads, mean_head, 0, unroll=4)

    def delta_head(h, table):
        cols = head_cols(h)
        delta = jnp.sum(dx[own, cols].astype(F32) * mean_v[:, cols], axis=1, keepdims=True)
        return jnp.where(lanes == h, delta, table)

    def send_delta():
        table = jnp.zeros((tile, 128), F32)
        for h in range(heads):
            table = delta_head(h, table)
        stat[...] = table.T
        dlt[:, own] = stat[0:16, :]
        for side, present, target, rows in sides:
            @pl.when(present)
            def _(side=side, target=target, rows=rows):
                small_copy(dlt.at[:, own], dlt, rows, side, dl_send, dl_recv, target).start()

    pl.when(is_first)(send_delta)
    for ordinal in range(3, 2 + GROUPS):
        start_static(ordinal)

    def transposed_head(h, carry):
        cols = head_cols(h)
        scores = scaling * nt(kx[own, cols], qx[:, cols]) - lsx[pl.ds(h, 1), :]
        left_flag = jnp.logical_and(flag(2, h) > 0, me > 0)
        right_flag = jnp.logical_and(flag(3, h) > 0, me < tiles - 1)
        left = jnp.where(left_flag, scores[:, :tile], LOW)
        right = jnp.where(right_flag, scores[:, 2 * tile:], LOW)
        scores = jnp.concatenate([left, scores[:, tile:2 * tile], right], axis=1)
        prob_t[h] = jnp.exp(scores)
        return carry

    @pl.when(jnp.logical_not(is_first))
    def _():
        for g in range(GROUPS):
            wait_static(2 + g)
        wait_small(lsx, ls_send, ls_recv)
        lax.fori_loop(0, heads, transposed_head, 0, unroll=4)
        weight_loads[0].wait()

    def hop_copy(n):
        return pltpu.make_async_remote_copy(
            src_ref=res.at[n], dst_ref=inx.at[n, own],
            send_sem=hop_send.at[n], recv_sem=hop_recv.at[n],
            device_id={"pipe": stage - 1}, device_id_type=MESH,
        )

    def wait_forwarded(n):
        for side, present, rows in here:
            @pl.when(present)
            def _(side=side, rows=rows):
                forward_chunk(n, 1 - side, {"seq": me}, rows).wait_recv()

    def accumulate_halo(n):
        wait_forwarded(n)
        accumulate(n, (low_rows, high_rows))

    for n in range(chunks):
        if n >= LAG:
            accumulate_halo(n - LAG)

        @pl.when(jnp.logical_not(is_first))
        def _(n=n):
            hop_copy(n).wait_recv()
            forward_all(n)
            accumulate(n, (own,))

    pl.when(jnp.logical_not(is_first))(send_delta)

    def query_head(h):
        cols = head_cols(h)
        d_own = dx[own, cols]
        delta = jnp.sum(d_own.astype(F32) * mean_v[:, cols], axis=1, keepdims=True)
        change = (prob[h] * (nt(d_own, vx[:, cols]) - delta)).astype(BF16)
        grad[0, :, cols] = (scaling * nn(change, kx[:, cols])).astype(BF16)

    for h in range(heads):
        query_head(h)
    for n in range(chunks - LAG, chunks):
        accumulate_halo(n)

    def key_head(h):
        cols = head_cols(h)
        grad[2, :, cols] = nn(prob_t[h].astype(BF16), dx[:, cols]).astype(BF16)
        change = (prob_t[h] * (nt(vx[own, cols], dx[:, cols]) - dlt[pl.ds(h, 1), :])).astype(BF16)
        grad[1, :, cols] = (scaling * nn(change, qx[:, cols])).astype(BF16)

    @pl.when(is_first)
    def _():
        wait_small(lsx, ls_send, ls_recv)
        wait_small(dlt, dl_send, dl_recv)
        for g in range(GROUPS):
            wait_static(2 + g)
            for h in range(g * group, (g + 1) * group):
                transposed_head(h, 0)
            for h in range(g * group, (g + 1) * group):
                key_head(h)

    @pl.when(jnp.logical_not(is_first))
    def _():
        wait_small(dlt, dl_send, dl_recv)
        for h in range(heads):
            key_head(h)

    for copy in weight_loads[1:]:
        copy.wait()

    for n in range(chunks):
        rows = pl.ds(n * CHUNK, CHUNK)
        total = inx[n, own, :].astype(F32) + nt(grad[0], wq[rows, :])
        total = total + nt(grad[1], wk[rows, :]) + nt(grad[2], wv[rows, :])
        total = total.astype(BF16)
        res[n] = total

        @pl.when(sends_on)
        def _(n=n):
            hop_copy(n).start()
        out_ref[0, :, rows] = total

    for side, present, target, rows in sides:
        @pl.when(present)
        def _(side=side, target=target, rows=rows):
            for ordinal, cols, source, into in statics:
                exchange(ordinal, side, target, rows, cols, source, into).wait_send()
            small_copy(lsx.at[:, own], lsx, rows, side, ls_send, ls_recv, target).wait_send()
            small_copy(dlt.at[:, own], dlt, rows, side, dl_send, dl_recv, target).wait_send()
            for n in range(chunks):
                forward_chunk(n, side, target, rows).wait_send()

    @pl.when(sends_on)
    def _():
        for n in range(chunks):
            hop_copy(n).wait_send()


def body(q, k, v, wq, wk, wv, wo, upstream, window):
    sections = lax.axis_size("pipe")
    tiles = window.shape[0]
    heads = window.shape[1]
    tile = q.shape[1]
    width = q.shape[2]
    model = upstream.shape[1]
    chunks = model // CHUNK
    hbm = pl.BlockSpec(memory_space=pl.ANY)
    vmem = pl.BlockSpec(memory_space=pltpu.VMEM)
    dma = pltpu.SemaphoreType.DMA
    return pl.pallas_call(
        functools.partial(relay_kernel, sections, tiles, heads, tile),
        out_shape=jax.ShapeDtypeStruct((1, tile, model), BF16),
        in_specs=[hbm] * 9,
        out_specs=vmem,
        scratch_shapes=[
            pltpu.VMEM((3 * tile, width), BF16),
            pltpu.VMEM((3 * tile, width), BF16),
            pltpu.VMEM((3 * tile, width), BF16),
            pltpu.VMEM((model, width), BF16),
            pltpu.VMEM((model, width), BF16),
            pltpu.VMEM((model, width), BF16),
            pltpu.VMEM((width, model), BF16),
            pltpu.VMEM((chunks, 3 * tile, CHUNK), BF16),
            pltpu.VMEM((3 * tile, width), F32),
            pltpu.VMEM((3 * tile, width), BF16),
            pltpu.VMEM((heads, tile, 3 * tile), F32),
            pltpu.VMEM((heads, tile, 3 * tile), F32),
            pltpu.VMEM((tile, width), F32),
            pltpu.VMEM((16, 3 * tile), F32),
            pltpu.VMEM((16, 3 * tile), F32),
            pltpu.VMEM((3, tile, width), BF16),
            pltpu.VMEM((chunks, tile, CHUNK), BF16),
            pltpu.VMEM((128, tile), F32),
            pltpu.VMEM((heads, 2, tiles), jnp.int32),
            pltpu.VMEM((4, 16, 128), F32),
            dma((4,)), dma((4,)), dma((chunks,)),
            dma((2 + GROUPS, 2)), dma((2 + GROUPS, 2)), dma((2,)), dma((2,)),
            dma((chunks,)), dma((chunks,)), dma((chunks, 2)), dma((chunks, 2)),
            dma((2,)), dma((2,)),
        ],
        compiler_params=pltpu.CompilerParams(
            collective_id=0, has_side_effects=True, vmem_limit_bytes=60 * 1024 * 1024
        ),
    )(q, k, v, wq, wk, wv, wo, upstream, jnp.transpose(window, (1, 2, 0)))


def solution(mesh):
    in_specs = (
        P("pipe", "seq", None),
        P("pipe", "seq", None),
        P("pipe", "seq", None),
        P("pipe", None, None),
        P("pipe", None, None),
        P("pipe", None, None),
        P("pipe", None, None),
        P("seq", None),
        P(),
    )
    out_specs = P("pipe", "seq", None)
    return jax.shard_map(body, mesh=mesh, in_specs=in_specs, out_specs=out_specs, check_vma=False)
```

```python
import functools

import jax
import jax.numpy as jnp
from jax import lax
from jax.experimental import pallas as pl
from jax.experimental.pallas import tpu as pltpu
from jax.sharding import PartitionSpec as P

HEAD_DIM = 128
COLUMN = 4
CHUNK = 256
LAG = 2
GROUPS = 3
MESH = pl.DeviceIdType.MESH
F32 = jnp.float32
BF16 = jnp.bfloat16
LOW = -1e30


def nt(a, b):
    return lax.dot_general(a, b, (((1,), (1,)), ((), ())), preferred_element_type=F32)


def nn(a, b):
    return lax.dot_general(a, b, (((1,), (0,)), ((), ())), preferred_element_type=F32)


def relay_kernel(
    sections, tiles, heads, tile,
    q_hbm, k_hbm, v_hbm, wq_hbm, wk_hbm, wv_hbm, wo_hbm, up_hbm, window_hbm,
    out_ref,
    qx, kx, vx, wq, wk, wv, wo, inx, acc, dx, prob, prob_t, mean_v, lsx, dlt, grad, res, stat, window, flags, part_k, part_v,
    load_sem, wsem, up_sem,
    kv_send, kv_recv, ls_send, ls_recv, hop_send, hop_recv, fwd_send, fwd_recv, dl_send, dl_recv,
):
    width = q_hbm.shape[2]
    model = up_hbm.shape[1]
    chunks = model // CHUNK
    scaling = HEAD_DIM ** (-0.5)
    stage = lax.axis_index("pipe")
    me = lax.axis_index("seq")
    has_left = jnp.logical_and(lax.rem(me, COLUMN) != COLUMN - 1, me > 0)
    has_right = jnp.logical_and(lax.rem(me, COLUMN) != COLUMN - 2, me < tiles - 1)
    is_first = stage == sections - 1
    sends_on = stage > 0
    own = pl.ds(tile, tile)
    low_rows = pl.ds(0, tile)
    high_rows = pl.ds(2 * tile, tile)
    sides = (
        (0, has_left, {"seq": me - 1}, high_rows),
        (1, has_right, {"seq": me + 1}, low_rows),
    )
    here = ((0, has_left, low_rows), (1, has_right, high_rows))

    barrier = pltpu.get_barrier_semaphore()
    for condition, target in (
        (has_left, {"seq": me - 1}),
        (has_right, {"seq": me + 1}),
        (sends_on, {"pipe": stage - 1}),
        (jnp.logical_not(is_first), {"pipe": stage + 1}),
    ):
        @pl.when(condition)
        def _(target=target):
            pl.semaphore_signal(barrier, inc=1, device_id=target, device_id_type=MESH)

    own_loads = [
        pltpu.make_async_copy(source.at[0], target.at[own], load_sem.at[n])
        for n, (source, target) in enumerate(((k_hbm, kx), (v_hbm, vx), (q_hbm, qx)))
    ]
    window_load = pltpu.make_async_copy(window_hbm, window, load_sem.at[3])
    window_load.start()
    for copy in own_loads:
        copy.start()
    weight_loads = [
        pltpu.make_async_copy(source.at[0], target, wsem.at[n])
        for n, (source, target) in enumerate(((wo_hbm, wo), (wq_hbm, wq), (wk_hbm, wk), (wv_hbm, wv)))
    ]
    for n in range(chunks):
        @pl.when(is_first)
        def _(n=n):
            pltpu.make_async_copy(
                up_hbm.at[:, pl.ds(n * CHUNK, CHUNK)], inx.at[n, own], up_sem.at[n]
            ).start()
    for copy in weight_loads:
        copy.start()

    for side, present, rows in here:
        @pl.when(jnp.logical_not(present))
        def _(side=side, rows=rows):
            for ref in (kx, vx, qx):
                ref[rows, :] = jnp.zeros((tile, width), BF16)
            for n in range(chunks):
                inx[n, rows, :] = jnp.zeros((tile, CHUNK), BF16)
            lsx[:, rows] = jnp.zeros((16, tile), F32)
            dlt[:, rows] = jnp.zeros((16, tile), F32)

    one = lambda flag: jnp.where(flag, 1, 0)
    pl.semaphore_wait(
        barrier,
        one(has_left) + one(has_right) + one(sends_on) + one(jnp.logical_not(is_first)),
    )

    def exchange(ordinal, side, target, rows, cols, source, into):
        return pltpu.make_async_remote_copy(
            src_ref=source.at[0, :, cols], dst_ref=into.at[rows, cols],
            send_sem=kv_send.at[ordinal, side], recv_sem=kv_recv.at[ordinal, side],
            device_id=target, device_id_type=MESH,
        )

    def forward_chunk(n, side, target, rows):
        return pltpu.make_async_remote_copy(
            src_ref=inx.at[n, own], dst_ref=inx.at[n, rows],
            send_sem=fwd_send.at[n, side], recv_sem=fwd_recv.at[n, side],
            device_id=target, device_id_type=MESH,
        )

    def forward_all(n):
        for side, present, target, rows in sides:
            @pl.when(present)
            def _(side=side, target=target, rows=rows):
                forward_chunk(n, side, target, rows).start()

    group = heads // GROUPS
    every = pl.ds(0, width)
    statics = [(0, every, k_hbm, kx), (1, every, v_hbm, vx)] + [
        (2 + g, pl.ds(g * group * HEAD_DIM, group * HEAD_DIM), q_hbm, qx) for g in range(GROUPS)
    ]

    def start_static(ordinal):
        _, cols, source, into = statics[ordinal]
        for side, present, target, rows in sides:
            @pl.when(present)
            def _(side=side, target=target, rows=rows):
                exchange(ordinal, side, target, rows, cols, source, into).start()

    start_static(0)
    start_static(1)

    @pl.when(is_first)
    def _():
        for n in range(chunks):
            pltpu.make_async_copy(
                up_hbm.at[:, pl.ds(n * CHUNK, CHUNK)], inx.at[n, own], up_sem.at[n]
            ).wait()
            forward_all(n)

    def wait_static(ordinal):
        _, cols, _, into = statics[ordinal]
        for side, present, rows in here:
            @pl.when(present)
            def _(side=side, rows=rows):
                pltpu.make_async_remote_copy(
                    src_ref=into.at[own, cols], dst_ref=into.at[rows, cols],
                    send_sem=kv_send.at[ordinal, 1 - side], recv_sem=kv_recv.at[ordinal, 1 - side],
                    device_id={"seq": me}, device_id_type=MESH,
                ).wait_recv()

    def small_copy(source, into, rows, side, send, recv, target):
        return pltpu.make_async_remote_copy(
            src_ref=source, dst_ref=into.at[:, rows],
            send_sem=send.at[side], recv_sem=recv.at[side],
            device_id=target, device_id_type=MESH,
        )

    def wait_small(into, send, recv):
        for side, present, rows in here:
            @pl.when(present)
            def _(side=side, rows=rows):
                small_copy(into.at[:, own], into, rows, 1 - side, send, recv, {"seq": me}).wait_recv()

    lanes = lax.broadcasted_iota(jnp.int32, (tile, 128), 1)

    def head_cols(h):
        if isinstance(h, int):
            return pl.ds(h * HEAD_DIM, HEAD_DIM)
        return pl.ds(pl.multiple_of(h * HEAD_DIM, HEAD_DIM), HEAD_DIM)

    def flag(kind, h):
        return flags[kind, pl.ds(h, 1), 0:1]

    before = jnp.maximum(me - 1, 0)
    after = jnp.minimum(me + 1, tiles - 1)

    def accumulate(n, row_sets):
        rows_in = [inx[n, rows, :] for rows in row_sets]
        incoming = rows_in[0] if len(rows_in) == 1 else jnp.concatenate(rows_in, axis=0)
        for m in range(width // CHUNK):
            out_cols = pl.ds(m * CHUNK, CHUNK)
            product = nt(incoming, wo[out_cols, pl.ds(n * CHUNK, CHUNK)])
            for i, rows in enumerate(row_sets):
                part = product[i * tile:(i + 1) * tile]
                if n > 0:
                    part = part + acc[rows, out_cols]
                if n == chunks - 1:
                    dx[rows, out_cols] = part.astype(BF16)
                else:
                    acc[rows, out_cols] = part

    @pl.when(is_first)
    def _():
        weight_loads[0].wait()
        for n in range(chunks):
            accumulate(n, (own,))

    window_load.wait()
    places = lax.broadcasted_iota(jnp.int32, (heads, tiles), 1)
    for kind, (index, which) in enumerate(((me, 0), (me, 1), (before, 1), (after, 0))):
        picked = jnp.where(places == index, window[:, which, :], 0).astype(F32)
        picked = jnp.sum(picked, axis=1, keepdims=True)
        flags[kind, 0:heads, :] = jnp.broadcast_to(picked, (heads, 128))

    for copy in own_loads:
        copy.wait()
    wait_static(0)

    def forward_head(h, table):
        cols = head_cols(h)
        scores = scaling * nt(qx[own, cols], kx[:, cols])
        left = jnp.where(flag(0, h) > 0, scores[:, :tile], LOW)
        right = jnp.where(flag(1, h) > 0, scores[:, 2 * tile:], LOW)
        scores = jnp.concatenate([left, scores[:, tile:2 * tile], right], axis=1)
        top = jnp.max(scores, axis=1, keepdims=True)
        powers = jnp.exp(scores - top)
        total = jnp.sum(powers, axis=1, keepdims=True)
        prob[h] = powers * (1.0 / total)
        return jnp.where(lanes == h, top + jnp.log(total), table)

    def mean_head(h, carry):
        cols = head_cols(h)
        weights = prob[h]
        high = weights.astype(BF16)
        rest = (weights - high.astype(F32)).astype(BF16)
        values = vx[:, cols]
        mean_v[:, cols] = nn(high, values) + nn(rest, values)
        return carry

    table = lax.fori_loop(0, heads, forward_head, jnp.zeros((tile, 128), F32), unroll=4)
    stat[...] = table.T
    lsx[:, own] = stat[0:16, :]
    for side, present, target, rows in sides:
        @pl.when(present)
        def _(side=side, target=target, rows=rows):
            small_copy(lsx.at[:, own], lsx, rows, side, ls_send, ls_recv, target).start()

    start_static(2)
    wait_static(1)
    lax.fori_loop(0, heads, mean_head, 0, unroll=4)

    def delta_head(h, table):
        cols = head_cols(h)
        delta = jnp.sum(dx[own, cols].astype(F32) * mean_v[:, cols], axis=1, keepdims=True)
        return jnp.where(lanes == h, delta, table)

    def send_delta():
        table = jnp.zeros((tile, 128), F32)
        for h in range(heads):
            table = delta_head(h, table)
        stat[...] = table.T
        dlt[:, own] = stat[0:16, :]
        for side, present, target, rows in sides:
            @pl.when(present)
            def _(side=side, target=target, rows=rows):
                small_copy(dlt.at[:, own], dlt, rows, side, dl_send, dl_recv, target).start()

    pl.when(is_first)(send_delta)
    for ordinal in range(3, 2 + GROUPS):
        start_static(ordinal)

    def transposed_head(h, carry):
        cols = head_cols(h)
        scores = scaling * nt(kx[own, cols], qx[:, cols]) - lsx[pl.ds(h, 1), :]
        left_flag = jnp.logical_and(flag(2, h) > 0, me > 0)
        right_flag = jnp.logical_and(flag(3, h) > 0, me < tiles - 1)
        left = jnp.where(left_flag, scores[:, :tile], LOW)
        right = jnp.where(right_flag, scores[:, 2 * tile:], LOW)
        scores = jnp.concatenate([left, scores[:, tile:2 * tile], right], axis=1)
        prob_t[h] = jnp.exp(scores)
        return carry

    @pl.when(jnp.logical_not(is_first))
    def _():
        for g in range(GROUPS):
            wait_static(2 + g)
        wait_small(lsx, ls_send, ls_recv)
        lax.fori_loop(0, heads, transposed_head, 0, unroll=4)
        weight_loads[0].wait()

    def hop_copy(n):
        return pltpu.make_async_remote_copy(
            src_ref=res.at[n], dst_ref=inx.at[n, own],
            send_sem=hop_send.at[n], recv_sem=hop_recv.at[n],
            device_id={"pipe": stage - 1}, device_id_type=MESH,
        )

    def wait_forwarded(n):
        for side, present, rows in here:
            @pl.when(present)
            def _(side=side, rows=rows):
                forward_chunk(n, 1 - side, {"seq": me}, rows).wait_recv()

    def accumulate_halo(n):
        wait_forwarded(n)
        accumulate(n, (low_rows, high_rows))

    for n in range(chunks):
        if n >= LAG:
            accumulate_halo(n - LAG)

        @pl.when(jnp.logical_not(is_first))
        def _(n=n):
            hop_copy(n).wait_recv()
            forward_all(n)
            accumulate(n, (own,))

    pl.when(jnp.logical_not(is_first))(send_delta)

    def query_head(h):
        cols = head_cols(h)
        d_own = dx[own, cols]
        delta = jnp.sum(d_own.astype(F32) * mean_v[:, cols], axis=1, keepdims=True)
        change = (prob[h] * (nt(d_own, vx[:, cols]) - delta)).astype(BF16)
        grad[0, :, cols] = (scaling * nn(change, kx[:, cols])).astype(BF16)

    for h in range(heads):
        query_head(h)

    def key_own(h):
        cols = head_cols(h)
        share = prob_t[h, :, own]
        d_own = dx[own, cols]
        part_v[:, cols] = nn(share.astype(BF16), d_own)
        change = (share * (nt(vx[own, cols], d_own) - dlt[pl.ds(h, 1), own])).astype(BF16)
        part_k[:, cols] = nn(change, qx[own, cols])

    def key_halo(h):
        cols = head_cols(h)
        outer = lambda ref: jnp.concatenate([ref[low_rows, cols], ref[high_rows, cols]], axis=0)
        share = jnp.concatenate([prob_t[h, :, low_rows], prob_t[h, :, high_rows]], axis=1)
        delta = jnp.concatenate([dlt[pl.ds(h, 1), low_rows], dlt[pl.ds(h, 1), high_rows]], axis=1)
        d_outer = outer(dx)
        grad[2, :, cols] = (part_v[:, cols] + nn(share.astype(BF16), d_outer)).astype(BF16)
        change = (share * (nt(vx[own, cols], d_outer) - delta)).astype(BF16)
        grad[1, :, cols] = (scaling * (part_k[:, cols] + nn(change, outer(qx)))).astype(BF16)

    @pl.when(jnp.logical_not(is_first))
    def _():
        for h in range(heads):
            key_own(h)

    for n in range(chunks - LAG, chunks):
        accumulate_halo(n)

    def key_head(h):
        cols = head_cols(h)
        grad[2, :, cols] = nn(prob_t[h].astype(BF16), dx[:, cols]).astype(BF16)
        change = (prob_t[h] * (nt(vx[own, cols], dx[:, cols]) - dlt[pl.ds(h, 1), :])).astype(BF16)
        grad[1, :, cols] = (scaling * nn(change, qx[:, cols])).astype(BF16)

    @pl.when(is_first)
    def _():
        wait_small(lsx, ls_send, ls_recv)
        wait_small(dlt, dl_send, dl_recv)
        for g in range(GROUPS):
            wait_static(2 + g)
            for h in range(g * group, (g + 1) * group):
                transposed_head(h, 0)
            for h in range(g * group, (g + 1) * group):
                key_head(h)

    @pl.when(jnp.logical_not(is_first))
    def _():
        wait_small(dlt, dl_send, dl_recv)
        for h in range(heads):
            key_halo(h)

    for copy in weight_loads[1:]:
        copy.wait()

    for n in range(chunks):
        rows = pl.ds(n * CHUNK, CHUNK)
        total = inx[n, own, :].astype(F32) + nt(grad[0], wq[rows, :])
        total = total + nt(grad[1], wk[rows, :]) + nt(grad[2], wv[rows, :])
        total = total.astype(BF16)
        res[n] = total

        @pl.when(sends_on)
        def _(n=n):
            hop_copy(n).start()
        out_ref[0, :, rows] = total

    for side, present, target, rows in sides:
        @pl.when(present)
        def _(side=side, target=target, rows=rows):
            for ordinal, cols, source, into in statics:
                exchange(ordinal, side, target, rows, cols, source, into).wait_send()
            small_copy(lsx.at[:, own], lsx, rows, side, ls_send, ls_recv, target).wait_send()
            small_copy(dlt.at[:, own], dlt, rows, side, dl_send, dl_recv, target).wait_send()
            for n in range(chunks):
                forward_chunk(n, side, target, rows).wait_send()

    @pl.when(sends_on)
    def _():
        for n in range(chunks):
            hop_copy(n).wait_send()


def body(q, k, v, wq, wk, wv, wo, upstream, window):
    sections = lax.axis_size("pipe")
    tiles = window.shape[0]
    heads = window.shape[1]
    tile = q.shape[1]
    width = q.shape[2]
    model = upstream.shape[1]
    chunks = model // CHUNK
    hbm = pl.BlockSpec(memory_space=pl.ANY)
    vmem = pl.BlockSpec(memory_space=pltpu.VMEM)
    dma = pltpu.SemaphoreType.DMA
    return pl.pallas_call(
        functools.partial(relay_kernel, sections, tiles, heads, tile),
        out_shape=jax.ShapeDtypeStruct((1, tile, model), BF16),
        in_specs=[hbm] * 9,
        out_specs=vmem,
        scratch_shapes=[
            pltpu.VMEM((3 * tile, width), BF16),
            pltpu.VMEM((3 * tile, width), BF16),
            pltpu.VMEM((3 * tile, width), BF16),
            pltpu.VMEM((model, width), BF16),
            pltpu.VMEM((model, width), BF16),
            pltpu.VMEM((model, width), BF16),
            pltpu.VMEM((width, model), BF16),
            pltpu.VMEM((chunks, 3 * tile, CHUNK), BF16),
            pltpu.VMEM((3 * tile, width), F32),
            pltpu.VMEM((3 * tile, width), BF16),
            pltpu.VMEM((heads, tile, 3 * tile), F32),
            pltpu.VMEM((heads, tile, 3 * tile), F32),
            pltpu.VMEM((tile, width), F32),
            pltpu.VMEM((16, 3 * tile), F32),
            pltpu.VMEM((16, 3 * tile), F32),
            pltpu.VMEM((3, tile, width), BF16),
            pltpu.VMEM((chunks, tile, CHUNK), BF16),
            pltpu.VMEM((128, tile), F32),
            pltpu.VMEM((heads, 2, tiles), jnp.int32),
            pltpu.VMEM((4, 16, 128), F32),
            pltpu.VMEM((tile, width), F32),
            pltpu.VMEM((tile, width), F32),
            dma((4,)), dma((4,)), dma((chunks,)),
            dma((2 + GROUPS, 2)), dma((2 + GROUPS, 2)), dma((2,)), dma((2,)),
            dma((chunks,)), dma((chunks,)), dma((chunks, 2)), dma((chunks, 2)),
            dma((2,)), dma((2,)),
        ],
        compiler_params=pltpu.CompilerParams(
            collective_id=0, has_side_effects=True, vmem_limit_bytes=60 * 1024 * 1024
        ),
    )(q, k, v, wq, wk, wv, wo, upstream, jnp.transpose(window, (1, 2, 0)))


def solution(mesh):
    in_specs = (
        P("pipe", "seq", None),
        P("pipe", "seq", None),
        P("pipe", "seq", None),
        P("pipe", None, None),
        P("pipe", None, None),
        P("pipe", None, None),
        P("pipe", None, None),
        P("seq", None),
        P(),
    )
    out_specs = P("pipe", "seq", None)
    return jax.shard_map(body, mesh=mesh, in_specs=in_specs, out_specs=out_specs, check_vma=False)
```

```python
import functools

import jax
import jax.numpy as jnp
from jax import lax
from jax.experimental import pallas as pl
from jax.experimental.pallas import tpu as pltpu
from jax.sharding import PartitionSpec as P

HEAD_DIM = 128
COLUMN = 4
CHUNK = 256
LAG = 2
GROUPS = 3
MESH = pl.DeviceIdType.MESH
F32 = jnp.float32
BF16 = jnp.bfloat16
LOW = -1e30


def nt(a, b):
    return lax.dot_general(a, b, (((1,), (1,)), ((), ())), preferred_element_type=F32)


def nn(a, b):
    return lax.dot_general(a, b, (((1,), (0,)), ((), ())), preferred_element_type=F32)


def relay_kernel(
    sections, tiles, heads, tile,
    q_hbm, k_hbm, v_hbm, wq_hbm, wk_hbm, wv_hbm, wo_hbm, up_hbm, window_hbm,
    out_ref,
    qx, kx, vx, wq, wk, wv, wo, inx, acc, dx, prob, prob_t, mean_v, lsx, dlt, grad, res, stat, window, flags, part_k, part_v,
    load_sem, wsem, up_sem,
    kv_send, kv_recv, ls_send, ls_recv, hop_send, hop_recv, fwd_send, fwd_recv, dl_send, dl_recv,
):
    width = q_hbm.shape[2]
    model = up_hbm.shape[1]
    chunks = model // CHUNK
    scaling = HEAD_DIM ** (-0.5)
    stage = lax.axis_index("pipe")
    me = lax.axis_index("seq")
    has_left = jnp.logical_and(lax.rem(me, COLUMN) != COLUMN - 1, me > 0)
    has_right = jnp.logical_and(lax.rem(me, COLUMN) != COLUMN - 2, me < tiles - 1)
    is_first = stage == sections - 1
    sends_on = stage > 0
    own = pl.ds(tile, tile)
    low_rows = pl.ds(0, tile)
    high_rows = pl.ds(2 * tile, tile)
    sides = (
        (0, has_left, {"seq": me - 1}, high_rows),
        (1, has_right, {"seq": me + 1}, low_rows),
    )
    here = ((0, has_left, low_rows), (1, has_right, high_rows))

    barrier = pltpu.get_barrier_semaphore()
    for condition, target in (
        (has_left, {"seq": me - 1}),
        (has_right, {"seq": me + 1}),
        (sends_on, {"pipe": stage - 1}),
        (jnp.logical_not(is_first), {"pipe": stage + 1}),
    ):
        @pl.when(condition)
        def _(target=target):
            pl.semaphore_signal(barrier, inc=1, device_id=target, device_id_type=MESH)

    own_loads = [
        pltpu.make_async_copy(source.at[0], target.at[own], load_sem.at[n])
        for n, (source, target) in enumerate(((k_hbm, kx), (v_hbm, vx), (q_hbm, qx)))
    ]
    window_load = pltpu.make_async_copy(window_hbm, window, load_sem.at[3])
    window_load.start()
    for copy in own_loads:
        copy.start()
    weight_loads = [
        pltpu.make_async_copy(source.at[0], target, wsem.at[n])
        for n, (source, target) in enumerate(((wo_hbm, wo), (wq_hbm, wq), (wk_hbm, wk), (wv_hbm, wv)))
    ]
    for n in range(chunks):
        @pl.when(is_first)
        def _(n=n):
            pltpu.make_async_copy(
                up_hbm.at[:, pl.ds(n * CHUNK, CHUNK)], inx.at[n, own], up_sem.at[n]
            ).start()
    for copy in weight_loads:
        copy.start()

    for side, present, rows in here:
        @pl.when(jnp.logical_not(present))
        def _(side=side, rows=rows):
            for ref in (kx, vx, qx):
                ref[rows, :] = jnp.zeros((tile, width), BF16)
            for n in range(chunks):
                inx[n, rows, :] = jnp.zeros((tile, CHUNK), BF16)
            lsx[:, rows] = jnp.zeros((16, tile), F32)
            dlt[:, rows] = jnp.zeros((16, tile), F32)

    one = lambda flag: jnp.where(flag, 1, 0)
    pl.semaphore_wait(
        barrier,
        one(has_left) + one(has_right) + one(sends_on) + one(jnp.logical_not(is_first)),
    )

    def exchange(ordinal, side, target, rows, cols, source, into):
        return pltpu.make_async_remote_copy(
            src_ref=source.at[0, :, cols], dst_ref=into.at[rows, cols],
            send_sem=kv_send.at[ordinal, side], recv_sem=kv_recv.at[ordinal, side],
            device_id=target, device_id_type=MESH,
        )

    def forward_chunk(n, side, target, rows):
        return pltpu.make_async_remote_copy(
            src_ref=inx.at[n, own], dst_ref=inx.at[n, rows],
            send_sem=fwd_send.at[n, side], recv_sem=fwd_recv.at[n, side],
            device_id=target, device_id_type=MESH,
        )

    def forward_all(n):
        for side, present, target, rows in sides:
            @pl.when(present)
            def _(side=side, target=target, rows=rows):
                forward_chunk(n, side, target, rows).start()

    group = heads // GROUPS
    every = pl.ds(0, width)
    statics = [(0, every, k_hbm, kx), (1, every, v_hbm, vx)] + [
        (2 + g, pl.ds(g * group * HEAD_DIM, group * HEAD_DIM), q_hbm, qx) for g in range(GROUPS)
    ]

    def start_static(ordinal):
        _, cols, source, into = statics[ordinal]
        for side, present, target, rows in sides:
            @pl.when(present)
            def _(side=side, target=target, rows=rows):
                exchange(ordinal, side, target, rows, cols, source, into).start()

    start_static(0)
    start_static(1)

    @pl.when(is_first)
    def _():
        for n in range(chunks):
            pltpu.make_async_copy(
                up_hbm.at[:, pl.ds(n * CHUNK, CHUNK)], inx.at[n, own], up_sem.at[n]
            ).wait()
            forward_all(n)

    def wait_static(ordinal):
        _, cols, _, into = statics[ordinal]
        for side, present, rows in here:
            @pl.when(present)
            def _(side=side, rows=rows):
                pltpu.make_async_remote_copy(
                    src_ref=into.at[own, cols], dst_ref=into.at[rows, cols],
                    send_sem=kv_send.at[ordinal, 1 - side], recv_sem=kv_recv.at[ordinal, 1 - side],
                    device_id={"seq": me}, device_id_type=MESH,
                ).wait_recv()

    def small_copy(source, into, rows, side, send, recv, target):
        return pltpu.make_async_remote_copy(
            src_ref=source, dst_ref=into.at[:, rows],
            send_sem=send.at[side], recv_sem=recv.at[side],
            device_id=target, device_id_type=MESH,
        )

    def wait_small(into, send, recv):
        for side, present, rows in here:
            @pl.when(present)
            def _(side=side, rows=rows):
                small_copy(into.at[:, own], into, rows, 1 - side, send, recv, {"seq": me}).wait_recv()

    lanes = lax.broadcasted_iota(jnp.int32, (tile, 128), 1)

    def head_cols(h):
        if isinstance(h, int):
            return pl.ds(h * HEAD_DIM, HEAD_DIM)
        return pl.ds(pl.multiple_of(h * HEAD_DIM, HEAD_DIM), HEAD_DIM)

    def flag(kind, h):
        return flags[kind, pl.ds(h, 1), 0:1]

    before = jnp.maximum(me - 1, 0)
    after = jnp.minimum(me + 1, tiles - 1)

    def accumulate(n, row_sets):
        rows_in = [inx[n, rows, :] for rows in row_sets]
        incoming = rows_in[0] if len(rows_in) == 1 else jnp.concatenate(rows_in, axis=0)
        for m in range(width // CHUNK):
            out_cols = pl.ds(m * CHUNK, CHUNK)
            product = nt(incoming, wo[out_cols, pl.ds(n * CHUNK, CHUNK)])
            for i, rows in enumerate(row_sets):
                part = product[i * tile:(i + 1) * tile]
                if n > 0:
                    part = part + acc[rows, out_cols]
                if n == chunks - 1:
                    dx[rows, out_cols] = part.astype(BF16)
                else:
                    acc[rows, out_cols] = part

    @pl.when(is_first)
    def _():
        weight_loads[0].wait()
        for n in range(chunks):
            accumulate(n, (own,))

    window_load.wait()
    places = lax.broadcasted_iota(jnp.int32, (heads, tiles), 1)
    for kind, (index, which) in enumerate(((me, 0), (me, 1), (before, 1), (after, 0))):
        picked = jnp.where(places == index, window[:, which, :], 0).astype(F32)
        picked = jnp.sum(picked, axis=1, keepdims=True)
        flags[kind, 0:heads, :] = jnp.broadcast_to(picked, (heads, 128))

    for copy in own_loads:
        copy.wait()
    wait_static(0)

    def forward_head(h, table):
        cols = head_cols(h)
        scores = scaling * nt(qx[own, cols], kx[:, cols])
        left = jnp.where(flag(0, h) > 0, scores[:, :tile], LOW)
        right = jnp.where(flag(1, h) > 0, scores[:, 2 * tile:], LOW)
        scores = jnp.concatenate([left, scores[:, tile:2 * tile], right], axis=1)
        top = jnp.max(scores, axis=1, keepdims=True)
        powers = jnp.exp(scores - top)
        total = jnp.sum(powers, axis=1, keepdims=True)
        prob[h] = powers * (1.0 / total)
        return jnp.where(lanes == h, top + jnp.log(total), table)

    def mean_head(h, carry):
        cols = head_cols(h)
        weights = prob[h]
        high = weights.astype(BF16)
        rest = (weights - high.astype(F32)).astype(BF16)
        values = vx[:, cols]
        mean_v[:, cols] = nn(high, values) + nn(rest, values)
        return carry

    table = lax.fori_loop(0, heads, forward_head, jnp.zeros((tile, 128), F32), unroll=4)
    stat[...] = table.T
    lsx[:, own] = stat[0:16, :]
    for side, present, target, rows in sides:
        @pl.when(present)
        def _(side=side, target=target, rows=rows):
            small_copy(lsx.at[:, own], lsx, rows, side, ls_send, ls_recv, target).start()

    start_static(2)
    wait_static(1)
    lax.fori_loop(0, heads, mean_head, 0, unroll=4)

    def delta_head(h, table):
        cols = head_cols(h)
        delta = jnp.sum(dx[own, cols].astype(F32) * mean_v[:, cols], axis=1, keepdims=True)
        return jnp.where(lanes == h, delta, table)

    def send_delta():
        table = jnp.zeros((tile, 128), F32)
        for h in range(heads):
            table = delta_head(h, table)
        stat[...] = table.T
        dlt[:, own] = stat[0:16, :]
        for side, present, target, rows in sides:
            @pl.when(present)
            def _(side=side, target=target, rows=rows):
                small_copy(dlt.at[:, own], dlt, rows, side, dl_send, dl_recv, target).start()

    pl.when(is_first)(send_delta)
    for ordinal in range(3, 2 + GROUPS):
        start_static(ordinal)

    def transposed_head(h, carry):
        cols = head_cols(h)
        scores = scaling * nt(kx[own, cols], qx[:, cols]) - lsx[pl.ds(h, 1), :]
        left_flag = jnp.logical_and(flag(2, h) > 0, me > 0)
        right_flag = jnp.logical_and(flag(3, h) > 0, me < tiles - 1)
        left = jnp.where(left_flag, scores[:, :tile], LOW)
        right = jnp.where(right_flag, scores[:, 2 * tile:], LOW)
        scores = jnp.concatenate([left, scores[:, tile:2 * tile], right], axis=1)
        prob_t[h] = jnp.exp(scores)
        return carry

    @pl.when(jnp.logical_not(is_first))
    def _():
        for g in range(GROUPS):
            wait_static(2 + g)
        wait_small(lsx, ls_send, ls_recv)
        lax.fori_loop(0, heads, transposed_head, 0, unroll=4)
        weight_loads[0].wait()

    def hop_copy(n):
        return pltpu.make_async_remote_copy(
            src_ref=res.at[n], dst_ref=inx.at[n, own],
            send_sem=hop_send.at[n], recv_sem=hop_recv.at[n],
            device_id={"pipe": stage - 1}, device_id_type=MESH,
        )

    def wait_forwarded(n):
        for side, present, rows in here:
            @pl.when(present)
            def _(side=side, rows=rows):
                forward_chunk(n, 1 - side, {"seq": me}, rows).wait_recv()

    def accumulate_halo(n):
        wait_forwarded(n)
        accumulate(n, (low_rows, high_rows))

    for n in range(chunks):
        @pl.when(jnp.logical_not(is_first))
        def _(n=n):
            hop_copy(n).wait_recv()
            forward_all(n)
            accumulate(n, (own,))

        if LAG <= n < chunks - 1:
            accumulate_halo(n - LAG)

    pl.when(jnp.logical_not(is_first))(send_delta)

    def query_head(h):
        cols = head_cols(h)
        d_own = dx[own, cols]
        delta = jnp.sum(d_own.astype(F32) * mean_v[:, cols], axis=1, keepdims=True)
        change = (prob[h] * (nt(d_own, vx[:, cols]) - delta)).astype(BF16)
        grad[0, :, cols] = (scaling * nn(change, kx[:, cols])).astype(BF16)

    for h in range(heads):
        query_head(h)

    def key_own(h):
        cols = head_cols(h)
        share = prob_t[h, :, own]
        d_own = dx[own, cols]
        part_v[:, cols] = nn(share.astype(BF16), d_own)
        change = (share * (nt(vx[own, cols], d_own) - dlt[pl.ds(h, 1), own])).astype(BF16)
        part_k[:, cols] = nn(change, qx[own, cols])

    def key_halo(h):
        cols = head_cols(h)
        outer = lambda ref: jnp.concatenate([ref[low_rows, cols], ref[high_rows, cols]], axis=0)
        share = jnp.concatenate([prob_t[h, :, low_rows], prob_t[h, :, high_rows]], axis=1)
        delta = jnp.concatenate([dlt[pl.ds(h, 1), low_rows], dlt[pl.ds(h, 1), high_rows]], axis=1)
        d_outer = outer(dx)
        grad[2, :, cols] = (part_v[:, cols] + nn(share.astype(BF16), d_outer)).astype(BF16)
        change = (share * (nt(vx[own, cols], d_outer) - delta)).astype(BF16)
        grad[1, :, cols] = (scaling * (part_k[:, cols] + nn(change, outer(qx)))).astype(BF16)

    @pl.when(jnp.logical_not(is_first))
    def _():
        for h in range(heads):
            key_own(h)

    for n in range(chunks - 1 - LAG, chunks):
        accumulate_halo(n)

    def key_head(h):
        cols = head_cols(h)
        grad[2, :, cols] = nn(prob_t[h].astype(BF16), dx[:, cols]).astype(BF16)
        change = (prob_t[h] * (nt(vx[own, cols], dx[:, cols]) - dlt[pl.ds(h, 1), :])).astype(BF16)
        grad[1, :, cols] = (scaling * nn(change, qx[:, cols])).astype(BF16)

    @pl.when(is_first)
    def _():
        wait_small(lsx, ls_send, ls_recv)
        wait_small(dlt, dl_send, dl_recv)
        for g in range(GROUPS):
            wait_static(2 + g)
            for h in range(g * group, (g + 1) * group):
                transposed_head(h, 0)
            for h in range(g * group, (g + 1) * group):
                key_head(h)

    @pl.when(jnp.logical_not(is_first))
    def _():
        wait_small(dlt, dl_send, dl_recv)
        for h in range(heads):
            key_halo(h)

    for copy in weight_loads[1:]:
        copy.wait()

    for n in range(chunks):
        rows = pl.ds(n * CHUNK, CHUNK)
        total = inx[n, own, :].astype(F32) + nt(grad[0], wq[rows, :])
        total = total + nt(grad[1], wk[rows, :]) + nt(grad[2], wv[rows, :])
        total = total.astype(BF16)
        res[n] = total

        @pl.when(sends_on)
        def _(n=n):
            hop_copy(n).start()
        out_ref[0, :, rows] = total

    for side, present, target, rows in sides:
        @pl.when(present)
        def _(side=side, target=target, rows=rows):
            for ordinal, cols, source, into in statics:
                exchange(ordinal, side, target, rows, cols, source, into).wait_send()
            small_copy(lsx.at[:, own], lsx, rows, side, ls_send, ls_recv, target).wait_send()
            small_copy(dlt.at[:, own], dlt, rows, side, dl_send, dl_recv, target).wait_send()
            for n in range(chunks):
                forward_chunk(n, side, target, rows).wait_send()

    @pl.when(sends_on)
    def _():
        for n in range(chunks):
            hop_copy(n).wait_send()


def body(q, k, v, wq, wk, wv, wo, upstream, window):
    sections = lax.axis_size("pipe")
    tiles = window.shape[0]
    heads = window.shape[1]
    tile = q.shape[1]
    width = q.shape[2]
    model = upstream.shape[1]
    chunks = model // CHUNK
    hbm = pl.BlockSpec(memory_space=pl.ANY)
    vmem = pl.BlockSpec(memory_space=pltpu.VMEM)
    dma = pltpu.SemaphoreType.DMA
    return pl.pallas_call(
        functools.partial(relay_kernel, sections, tiles, heads, tile),
        out_shape=jax.ShapeDtypeStruct((1, tile, model), BF16),
        in_specs=[hbm] * 9,
        out_specs=vmem,
        scratch_shapes=[
            pltpu.VMEM((3 * tile, width), BF16),
            pltpu.VMEM((3 * tile, width), BF16),
            pltpu.VMEM((3 * tile, width), BF16),
            pltpu.VMEM((model, width), BF16),
            pltpu.VMEM((model, width), BF16),
            pltpu.VMEM((model, width), BF16),
            pltpu.VMEM((width, model), BF16),
            pltpu.VMEM((chunks, 3 * tile, CHUNK), BF16),
            pltpu.VMEM((3 * tile, width), F32),
            pltpu.VMEM((3 * tile, width), BF16),
            pltpu.VMEM((heads, tile, 3 * tile), F32),
            pltpu.VMEM((heads, tile, 3 * tile), F32),
            pltpu.VMEM((tile, width), F32),
            pltpu.VMEM((16, 3 * tile), F32),
            pltpu.VMEM((16, 3 * tile), F32),
            pltpu.VMEM((3, tile, width), BF16),
            pltpu.VMEM((chunks, tile, CHUNK), BF16),
            pltpu.VMEM((128, tile), F32),
            pltpu.VMEM((heads, 2, tiles), jnp.int32),
            pltpu.VMEM((4, 16, 128), F32),
            pltpu.VMEM((tile, width), F32),
            pltpu.VMEM((tile, width), F32),
            dma((4,)), dma((4,)), dma((chunks,)),
            dma((2 + GROUPS, 2)), dma((2 + GROUPS, 2)), dma((2,)), dma((2,)),
            dma((chunks,)), dma((chunks,)), dma((chunks, 2)), dma((chunks, 2)),
            dma((2,)), dma((2,)),
        ],
        compiler_params=pltpu.CompilerParams(
            collective_id=0, has_side_effects=True, vmem_limit_bytes=60 * 1024 * 1024
        ),
    )(q, k, v, wq, wk, wv, wo, upstream, jnp.transpose(window, (1, 2, 0)))


def solution(mesh):
    in_specs = (
        P("pipe", "seq", None),
        P("pipe", "seq", None),
        P("pipe", "seq", None),
        P("pipe", None, None),
        P("pipe", None, None),
        P("pipe", None, None),
        P("pipe", None, None),
        P("seq", None),
        P(),
    )
    out_specs = P("pipe", "seq", None)
    return jax.shard_map(body, mesh=mesh, in_specs=in_specs, out_specs=out_specs, check_vma=False)
```
